128 devices in a mesh: chi: 2 (over core), phi: 64 (over z, y, x).
Axes of the slice: x: 4, y: 4, z: 4, core: 2. Of those that a mesh axis runs over, the one named last changes fastest.
Arguments:
- frames: bfloat16 [1024, 8, 8, 2048], P('phi', 'chi'), may hold values from 0.25 to 8
- drift_rows: int32 [1024, 8], P('phi', 'chi'), may hold values from -2 to 2
- drift_cols: int32 [1024, 8], P('phi', 'chi'), may hold values from -24 to 24
- weight_index: int32 [1024, 8], P('phi', 'chi'), may hold values from 0 to 63
- blur_band: int32 [16384], P('chi'), may hold values from 0 to 3
Outputs:
- restored: float32 [1024, 8, 16384], P('phi', None, 'chi')
The draws below stay inside these ranges and needn't reach their ends.
All inputs are finite; a program needn't handle non-finite values.
Results may differ from the reference program's by a relative error of at most 0.0003.
Values sent between devices are 32-bit elements; how exact they have to be, the bound alone decides.
A program may use at most 128 MiB of HBM per device.

```python
import math
import jax
import jax.numpy as jnp
from jax import lax

ROWS = 8
COLS = 2048
ITERS = 3
CHI = 1024
PHI = 8
PIX = 16384
N_CHI = 2


def touch_ends(values, key, smallest, high):
    place = [jax.random.randint(jax.random.fold_in(key, axis), (), 0, length) for axis, length in enumerate(values.shape)]
    longest = values.shape.index(max(values.shape))
    next_to = place[:longest] + [(place[longest] + 1) % values.shape[longest]] + place[longest + 1:]
    return values.at[tuple(place)].set(smallest).at[tuple(next_to)].set(high)


def steps_of(own_key, extent, pieces, low, high):
    def one(axis_at, shards_of):
        steps = jax.random.uniform(jax.random.fold_in(jax.random.fold_in(own_key, 6), axis_at), (shards_of,), jnp.float32, low / len(pieces), high / len(pieces))
        return jnp.repeat(jnp.exp(steps), extent[axis_at] // shards_of).reshape((-1,) + (1,) * (len(extent) - axis_at - 1))

    factor_of = one(*pieces[0])
    for cut in pieces[1:]:
        factor_of = factor_of * one(*cut)
    return factor_of


def setup_inputs(seed: int = 0) -> dict:
    seeds = jax.random.split(jax.random.key(seed), 6)
    return {
        "frames": jnp.clip(jnp.exp(math.log(8.0) - 3.465736 * jax.random.uniform(seeds[0], (CHI, PHI, ROWS, COLS), jnp.float32) ** steps_of(seeds[0], (CHI, PHI, ROWS, COLS), ((0, 64), (1, 2)), -0.2, 0.2)), 0.25, 8.0).astype(jnp.bfloat16),
        "drift_rows": touch_ends(jax.random.randint(seeds[1], (CHI, PHI), -2, 3), jax.random.fold_in(seeds[1], 1), -2, 2).astype(jnp.int32),
        "drift_cols": touch_ends(jax.random.randint(seeds[2], (CHI, PHI), -24, 25), jax.random.fold_in(seeds[2], 1), -24, 24).astype(jnp.int32),
        "weight_index": touch_ends(jax.random.randint(seeds[3], (CHI, PHI), 0, 64), jax.random.fold_in(seeds[3], 1), 0, 63).astype(jnp.int32),
        "blur_band": touch_ends(jax.random.randint(seeds[4], (PIX,), 0, 4), jax.random.fold_in(seeds[4], 1), 0, 3).astype(jnp.int32),
    }


def shift_one(frame, row_drift, col_drift, table_index):
    padded = jnp.pad(frame.astype(jnp.float32), ((3, 3), (25, 25)))
    frac_y = (table_index // 8).astype(jnp.float32) / 8.0
    frac_x = (table_index % 8).astype(jnp.float32) / 8.0
    summed = jnp.zeros(frame.shape, jnp.float32)
    for a in range(2):
        for b in range(2):
            factor = (frac_y if a else 1.0 - frac_y) * (frac_x if b else 1.0 - frac_x)
            start_row = (3 - row_drift - a).astype(jnp.int32)
            start_col = (25 - col_drift - b).astype(jnp.int32)
            window = lax.dynamic_slice(padded, (start_row, start_col), frame.shape)
            summed = summed + factor * window
    return summed.reshape(-1)


def tap_weights(band_index):
    spread = 0.8 + 0.6 * band_index.astype(jnp.float32)
    offsets = jnp.arange(-4, 5).astype(jnp.float32)
    unnormed = jnp.exp(-(offsets[:, None] ** 2) / (2.0 * spread[None, :] ** 2))
    return unnormed / jnp.sum(unnormed, axis=0, keepdims=True)


def blur_tilts(extended, weights):
    number = extended.shape[1]
    padded = jnp.pad(extended, ((0, 0), (4, 4), (0, 0)))
    phi_sum = jnp.zeros(extended.shape, jnp.float32)
    for k in range(9):
        phi_sum = phi_sum + weights[k][None, None, :] * padded[:, k:k + number, :]
    return 0.25 * phi_sum[:-2] + 0.5 * phi_sum[1:-1] + 0.25 * phi_sum[2:]


def deblur(data, weights):
    estimate = data + 0.1
    for iteration in range(ITERS):
        blurred = blur_tilts(jnp.pad(estimate, ((1, 1), (0, 0), (0, 0))), weights)
        ratio = data / (blurred + 0.1)
        estimate = estimate * blur_tilts(jnp.pad(ratio, ((1, 1), (0, 0), (0, 0))), weights)
    return estimate


def reference(frames, drift_rows, drift_cols, weight_index, blur_band):
    def per_chi(members):
        return jax.vmap(shift_one)(*members)

    data = lax.map(per_chi, (frames, drift_rows, drift_cols, weight_index))
    weights = tap_weights(blur_band)
    block_size = PIX // N_CHI
    block_count = PIX // block_size

    def per_block(number):
        first = (number * block_size).astype(jnp.int32)
        window = lax.dynamic_slice_in_dim(data, first, block_size, 2)
        sub_weights = lax.dynamic_slice_in_dim(weights, first, block_size, 1)
        return deblur(window, sub_weights)

    blocks = lax.map(per_block, jnp.arange(block_count).astype(jnp.int32))
    return jnp.transpose(blocks, (1, 2, 0, 3)).reshape(CHI, PHI, PIX)
```

```python
import functools

import jax
import jax.numpy as jnp
from jax import lax
from jax.experimental import pallas as pl
from jax.experimental.pallas import tpu as pltpu
from jax.sharding import PartitionSpec as P

ITERS = 3
HALO = 2 * ITERS
LANES = 128
SUBS = 8
PAD_ROWS = 3
REMOTE = 4


def shift_tilt(tilt, rows_ref, cols_ref, index_ref, frames_ref, spread_ref, staged_ref):
    own_phis, rows, cols = frames_ref.shape[1:]
    tiles = cols // LANES
    halves = tiles // SUBS
    blocks = staged_ref.shape[1]
    lane = lax.broadcasted_iota(jnp.int32, (rows, LANES), 1)
    zero = jnp.zeros((rows, LANES), jnp.float32)
    for p in range(own_phis):
        drift_col = cols_ref[tilt, p]
        frac_x = (index_ref[tilt, p] & 7).astype(jnp.float32) / 8.0
        turn = (drift_col + LANES) & (LANES - 1)
        from_left = lane < drift_col
        from_right = lane >= LANES + drift_col
        frame = frames_ref[tilt, p].astype(jnp.float32)
        source = [frame[:, t * LANES : (t + 1) * LANES] for t in range(tiles)] + [zero]
        stepped = [pltpu.roll(s, 1, 1) for s in source[:-1]]
        turned = []
        for t in range(tiles + 1):
            before = stepped[t - 1] if t > 0 else zero
            here = stepped[t] if t < tiles else zero
            mixed = (1.0 - frac_x) * source[t] + frac_x * jnp.where(lane < 1, before, here)
            turned.append(pltpu.roll(mixed, turn, 1))
        moved = []
        for t in range(tiles):
            left = turned[t - 1] if t > 0 else zero
            moved.append(jnp.where(from_left, left, jnp.where(from_right, turned[t + 1], turned[t])))
        for h in range(halves):
            group = jnp.stack(moved[h * SUBS : (h + 1) * SUBS])
            spread_ref[p, PAD_ROWS : PAD_ROWS + rows, h] = jnp.swapaxes(group, 0, 1)
    for p in range(own_phis):
        drift_row = rows_ref[tilt, p]
        frac_y = (index_ref[tilt, p] >> 3).astype(jnp.float32) / 8.0
        for r in range(rows):
            row = (1.0 - frac_y) * spread_ref[p, r + PAD_ROWS - drift_row] + frac_y * spread_ref[
                p, r + PAD_ROWS - 1 - drift_row
            ]
            for h in range(halves):
                place = r * halves + h
                staged_ref[place // blocks, place % blocks, tilt, p] = row[h]


def tap_matrices(band):
    spread = 0.8 + 0.6 * band.astype(jnp.float32)
    unnormed = [jnp.exp(-float(k * k) / (2.0 * spread * spread)) for k in range(5)]
    total = unnormed[0] + 2.0 * (unnormed[1] + unnormed[2] + unnormed[3] + unnormed[4])
    taps = [0.125 * (u / total) for u in unnormed]
    made = {}

    def pair(near, far, sign):
        if far > 4:
            return taps[near]
        if (near, far, sign) not in made:
            made[near, far, sign] = taps[near] + sign * taps[far] if near < far else taps[near] * 1.0 + sign * taps[far]
        return made[near, far, sign]

    even = [[pair(abs(p - q), 7 - p - q, 1.0) for q in range(4)] for p in range(4)]
    odd = [[pair(abs(p - q), 7 - p - q, -1.0) for q in range(4)] for p in range(4)]
    return even, odd


def phi_blur(tilts, even, odd):
    plus = [tilts[p] + tilts[7 - p] for p in range(4)]
    minus = [tilts[p] - tilts[7 - p] for p in range(4)]
    halves = []
    for matrix, parts in ((even, plus), (odd, minus)):
        rows = []
        for p in range(4):
            row = matrix[p][0] * parts[0]
            for q in range(1, 4):
                row = row + matrix[p][q] * parts[q]
            rows.append(row)
        halves.append(rows)
    front = [halves[0][p] + halves[1][p] for p in range(4)]
    back = [halves[0][3 - p] - halves[1][3 - p] for p in range(4)]
    return front + back


def sweep(load, emit, low, high, even, odd):
    before = phi_blur(load(low - 1), even, odd)
    here = phi_blur(load(low), even, odd)
    joined = [a + b for a, b in zip(before, here)]

    def step(c, carry):
        here, joined = carry
        after = phi_blur(load(c + 1), even, odd)
        ahead = [a + b for a, b in zip(here, after)]
        emit(c, [a + b for a, b in zip(joined, ahead)])
        return after, ahead

    lax.fori_loop(low, high, step, (here, joined), unroll=2)


def kernel(
    n_phi,
    rows_ref,
    cols_ref,
    index_ref,
    band_ref,
    frames_hbm,
    out_hbm,
    frames_ref,
    spread_ref,
    staged_ref,
    data_ref,
    estimate_ref,
    ratio_ref,
    done_ref,
    frame_sems,
    send_sems,
    recv_sems,
    pair_sends,
    pair_recvs,
    local_sems,
    out_sems,
):
    chi, phi = lax.axis_index("chi"), lax.axis_index("phi")
    other = 1 - chi
    before = lax.rem(phi + n_phi - 1, n_phi)
    after = lax.rem(phi + 1, n_phi)
    own_tilts, own_phis = frames_ref.shape[:2]
    blocks, all_tilts, phis = data_ref.shape[:3]
    sizes = (HALO, HALO, own_tilts - 2 * HALO)
    firsts = (0, own_tilts - HALO, HALO)

    loads = []
    for number, (first, size) in enumerate(zip(firsts, sizes)):
        part = pl.ds(first, size)
        loads.append(pltpu.make_async_copy(frames_hbm.at[part], frames_ref.at[part], frame_sems.at[number]))
        loads[-1].start()

    barrier = pltpu.get_barrier_semaphore()
    peers = [(before, 0), (before, 1), (after, 0), (after, 1)]
    for to_phi, to_chi in peers + [(phi, other)]:
        pl.semaphore_signal(
            barrier, inc=1, device_id={"chi": to_chi, "phi": to_phi}, device_id_type=pl.DeviceIdType.MESH
        )

    empty = jnp.zeros(spread_ref.shape[2:], jnp.float32)
    for p in range(own_phis):
        for r in range(PAD_ROWS):
            spread_ref[p, r] = empty
            spread_ref[p, spread_ref.shape[1] - 1 - r] = empty

    def shift_tilts(first, size):
        def step(tilt, carry):
            shift_tilt(tilt, rows_ref, cols_ref, index_ref, frames_ref, spread_ref, staged_ref)
            return carry

        lax.fori_loop(first, first + size, step, 0)

    mine = pl.ds(chi * own_phis, own_phis)

    def neighbour_copy(b, number):
        to_phi, to_chi = peers[number]
        back = number < 2
        from_tilts = pl.ds(0 if back else own_tilts - HALO, HALO)
        to_tilts = pl.ds(all_tilts - HALO if back else 0, HALO)
        place = (0 if back else 2) + chi
        return pltpu.make_async_remote_copy(
            src_ref=staged_ref.at[to_chi, b, from_tilts],
            dst_ref=data_ref.at[b, to_tilts, mine],
            send_sem=send_sems.at[b, number],
            recv_sem=recv_sems.at[b, place],
            device_id={"chi": to_chi, "phi": to_phi},
            device_id_type=pl.DeviceIdType.MESH,
        )

    def arrival(b, place):
        back = place < 2
        to_tilts = pl.ds(all_tilts - HALO if back else 0, HALO)
        from_chi = place % 2
        return pltpu.make_async_remote_copy(
            src_ref=staged_ref.at[0, b, pl.ds(0, HALO)],
            dst_ref=data_ref.at[b, to_tilts, pl.ds(from_chi * own_phis, own_phis)],
            send_sem=send_sems.at[b, place],
            recv_sem=recv_sems.at[b, place],
            device_id={"chi": from_chi, "phi": after if back else before},
            device_id_type=pl.DeviceIdType.MESH,
        )

    middle = pl.ds(HALO, own_tilts)

    def pair_copy(b, phis_at):
        return pltpu.make_async_remote_copy(
            src_ref=staged_ref.at[other, b],
            dst_ref=data_ref.at[b, middle, phis_at],
            send_sem=pair_sends.at[b],
            recv_sem=pair_recvs.at[b],
            device_id={"chi": other, "phi": phi},
            device_id_type=pl.DeviceIdType.MESH,
        )

    def local_copy(b):
        return pltpu.make_async_copy(staged_ref.at[chi, b], data_ref.at[b, middle, mine], local_sems.at[b])

    loads[0].wait()
    shift_tilts(firsts[0], sizes[0])
    loads[1].wait()
    shift_tilts(firsts[1], sizes[1])
    pl.semaphore_wait(barrier, len(peers) + 1)

    def send_halos(b, carry):
        for number in range(REMOTE):
            neighbour_copy(b, number).start()
        return carry

    lax.fori_loop(0, blocks, send_halos, 0)
    loads[2].wait()
    shift_tilts(firsts[2], sizes[2])

    def send_pairs(b, carry):
        pair_copy(b, mine).start()
        local_copy(b).start()
        return carry

    lax.fori_loop(0, blocks, send_pairs, 0)

    left_add = jnp.where(phi == 0, 0.0, 0.1)
    right_add = jnp.where(phi == n_phi - 1, 0.0, 0.1)

    def out_copy(b, p):
        return pltpu.make_async_copy(
            done_ref.at[b, :, p], out_hbm.at[:, pl.ds(b * SUBS, SUBS), p, :], out_sems.at[b, p]
        )

    def block(b, carry):
        for place in range(REMOTE):
            arrival(b, place).wait_recv()
        pair_copy(b, pl.ds(other * own_phis, own_phis)).wait_recv()
        local_copy(b).wait()
        nothing = jnp.zeros((HALO,) + data_ref.shape[2:], jnp.float32)

        @pl.when(phi == 0)
        def _():
            data_ref[b, 0:HALO] = nothing

        @pl.when(phi == n_phi - 1)
        def _():
            data_ref[b, all_tilts - HALO : all_tilts] = nothing

        even, odd = tap_matrices(band_ref[pl.ds(pl.multiple_of(b * SUBS, SUBS), SUBS), :])

        def start(c):
            add = jnp.where(c < HALO, left_add, jnp.where(c >= HALO + own_tilts, right_add, 0.1))
            return [data_ref[b, c, p] + add for p in range(phis)]

        def held(c):
            return [estimate_ref[c, p] for p in range(phis)]

        def ratios(c):
            return [ratio_ref[c, p] for p in range(phis)]

        for iteration in range(ITERS):
            estimate = start if iteration == 0 else held
            margin = 2 * iteration + 1

            def to_ratio(c, blurred):
                for p in range(phis):
                    ratio_ref[c, p] = data_ref[b, c, p] / (blurred[p] + 0.1)

            def to_estimate(c, factor):
                old = estimate(c)
                for p in range(phis):
                    if iteration == ITERS - 1:
                        done_ref[b, c - HALO, p] = old[p] * factor[p]
                    else:
                        estimate_ref[c, p] = old[p] * factor[p]

            sweep(estimate, to_ratio, margin, all_tilts - margin, even, odd)
            sweep(ratios, to_estimate, margin + 1, all_tilts - margin - 1, even, odd)
        for p in range(phis):
            out_copy(b, p).start()
        return carry

    lax.fori_loop(0, blocks, block, 0)

    def finish(b, carry):
        for number in range(REMOTE):
            neighbour_copy(b, number).wait_send()
        pair_copy(b, mine).wait_send()
        for p in range(phis):
            out_copy(b, p).wait()
        return carry

    lax.fori_loop(0, blocks, finish, 0)


def body(n_phi, frames, drift_rows, drift_cols, weight_index, blur_band):
    tilts, own_phis, rows, cols = frames.shape
    pixels = blur_band.shape[0]
    phis = 2 * own_phis
    planes = pixels // LANES
    blocks = planes // SUBS
    tile = (SUBS, LANES)
    all_tilts = tilts + 2 * HALO
    smem = pl.BlockSpec(memory_space=pltpu.SMEM)
    vmem = pl.BlockSpec(memory_space=pltpu.VMEM)
    out = pl.pallas_call(
        functools.partial(kernel, n_phi),
        out_shape=jax.ShapeDtypeStruct((tilts, planes, phis, LANES), jnp.float32),
        in_specs=[smem, smem, smem, vmem, pl.BlockSpec(memory_space=pl.ANY)],
        out_specs=pl.BlockSpec(memory_space=pl.ANY),
        scratch_shapes=[
            pltpu.VMEM(frames.shape, frames.dtype),
            pltpu.VMEM((own_phis, rows + 2 * PAD_ROWS, cols // LANES // SUBS) + tile, jnp.float32),
            pltpu.VMEM((2, blocks, tilts, own_phis) + tile, jnp.float32),
            pltpu.VMEM((blocks, all_tilts, phis) + tile, jnp.float32),
            pltpu.VMEM((all_tilts, phis) + tile, jnp.float32),
            pltpu.VMEM((all_tilts, phis) + tile, jnp.float32),
            pltpu.VMEM((blocks, tilts, phis) + tile, jnp.float32),
            pltpu.SemaphoreType.DMA((3,)),
            pltpu.SemaphoreType.DMA((blocks, REMOTE)),
            pltpu.SemaphoreType.DMA((blocks, REMOTE)),
            pltpu.SemaphoreType.DMA((blocks,)),
            pltpu.SemaphoreType.DMA((blocks,)),
            pltpu.SemaphoreType.DMA((blocks,)),
            pltpu.SemaphoreType.DMA((blocks, phis)),
        ],
        compiler_params=pltpu.CompilerParams(
            collective_id=0, has_side_effects=True, vmem_limit_bytes=48 * 1024 * 1024
        ),
        name="rocking",
    )(drift_rows, drift_cols, weight_index, blur_band.reshape(planes, LANES), frames)
    return out.transpose(0, 2, 1, 3).reshape(tilts, phis, pixels)


def solution(mesh):
    return jax.shard_map(
        functools.partial(body, mesh.shape["phi"]),
        mesh=mesh,
        in_specs=(
            P("phi", "chi", None, None),
            P("phi", "chi"),
            P("phi", "chi"),
            P("phi", "chi"),
            P("chi"),
        ),
        out_specs=P("phi", None, "chi"),
        check_vma=False,
    )
```

```python
import functools

import jax
import jax.numpy as jnp
from jax import lax
from jax.experimental import pallas as pl
from jax.experimental.pallas import tpu as pltpu
from jax.sharding import PartitionSpec as P

ITERS = 3
HALO = 2 * ITERS
LANES = 128
SUBS = 8
MOST_ROWS = 2
PAD_ROWS = MOST_ROWS + 1
REMOTE = 4


def shift_tilt(tilt, rows_ref, cols_ref, index_ref, frames_ref, spread_ref, staged_ref):
    own_phis, rows, cols = frames_ref.shape[1:]
    tiles = cols // LANES
    halves = tiles // SUBS
    blocks = staged_ref.shape[1]
    lane = lax.broadcasted_iota(jnp.int32, (rows, LANES), 1)
    zero = jnp.zeros((rows, LANES), jnp.float32)
    for p in range(own_phis):
        drift_col = cols_ref[p, tilt]
        frac_x = (index_ref[p, tilt] & 7).astype(jnp.float32) / 8.0
        turn = (drift_col + LANES) & (LANES - 1)
        from_left = lane < drift_col
        from_right = lane >= LANES + drift_col
        frame = frames_ref[tilt, p].astype(jnp.float32)
        source = [frame[:, t * LANES : (t + 1) * LANES] for t in range(tiles)] + [zero]
        stepped = [pltpu.roll(s, 1, 1) for s in source[:-1]]
        turned = []
        for t in range(tiles + 1):
            before = stepped[t - 1] if t > 0 else zero
            here = stepped[t] if t < tiles else zero
            mixed = (1.0 - frac_x) * source[t] + frac_x * jnp.where(lane < 1, before, here)
            turned.append(pltpu.roll(mixed, turn, 1))
        moved = []
        for t in range(tiles):
            left = turned[t - 1] if t > 0 else zero
            moved.append(jnp.where(from_left, left, jnp.where(from_right, turned[t + 1], turned[t])))
        for h in range(halves):
            group = jnp.stack(moved[h * SUBS : (h + 1) * SUBS])
            spread_ref[p, PAD_ROWS : PAD_ROWS + rows, h] = jnp.swapaxes(group, 0, 1)
    for p in range(own_phis):
        drift_row = rows_ref[p, tilt]
        frac_y = (index_ref[p, tilt] >> 3).astype(jnp.float32) / 8.0
        for r in range(rows):
            row = (1.0 - frac_y) * spread_ref[p, r + PAD_ROWS - drift_row] + frac_y * spread_ref[
                p, r + PAD_ROWS - 1 - drift_row
            ]
            for h in range(halves):
                place = r * halves + h
                staged_ref[place // blocks, place % blocks, tilt, p] = row[h]


def tap_matrices(band):
    spread = 0.8 + 0.6 * band.astype(jnp.float32)
    unnormed = [jnp.exp(-float(k * k) / (2.0 * spread * spread)) for k in range(5)]
    total = unnormed[0] + 2.0 * (unnormed[1] + unnormed[2] + unnormed[3] + unnormed[4])
    taps = [0.125 * (u / total) for u in unnormed]
    made = {}

    def pair(near, far, sign):
        if far > 4:
            return taps[near]
        if (near, far, sign) not in made:
            made[near, far, sign] = taps[near] + sign * taps[far] if near < far else taps[near] * 1.0 + sign * taps[far]
        return made[near, far, sign]

    even = [[pair(abs(p - q), 7 - p - q, 1.0) for q in range(4)] for p in range(4)]
    odd = [[pair(abs(p - q), 7 - p - q, -1.0) for q in range(4)] for p in range(4)]
    return even, odd


def phi_blur(tilts, even, odd):
    plus = [tilts[p] + tilts[7 - p] for p in range(4)]
    minus = [tilts[p] - tilts[7 - p] for p in range(4)]
    halves = []
    for matrix, parts in ((even, plus), (odd, minus)):
        rows = []
        for p in range(4):
            row = matrix[p][0] * parts[0]
            for q in range(1, 4):
                row = row + matrix[p][q] * parts[q]
            rows.append(row)
        halves.append(rows)
    front = [halves[0][p] + halves[1][p] for p in range(4)]
    back = [halves[0][3 - p] - halves[1][3 - p] for p in range(4)]
    return front + back


def sweep(load, emit, low, high, even, odd):
    before = phi_blur(load(low - 1), even, odd)
    here = phi_blur(load(low), even, odd)
    joined = [a + b for a, b in zip(before, here)]

    def step(c, carry):
        here, joined = carry
        after = phi_blur(load(c + 1), even, odd)
        ahead = [a + b for a, b in zip(here, after)]
        emit(c, [a + b for a, b in zip(joined, ahead)])
        return after, ahead

    lax.fori_loop(low, high, step, (here, joined), unroll=2)


def kernel(
    n_phi,
    rows_ref,
    cols_ref,
    index_ref,
    band_hbm,
    frames_hbm,
    out_ref,
    band_ref,
    frames_ref,
    spread_ref,
    staged_ref,
    data_ref,
    estimate_ref,
    ratio_ref,
    band_sem,
    frame_sems,
    send_sems,
    recv_sems,
    pair_sends,
    pair_recvs,
    local_sems,
):
    chi, phi = lax.axis_index("chi"), lax.axis_index("phi")
    other = 1 - chi
    before = lax.rem(phi + n_phi - 1, n_phi)
    after = lax.rem(phi + 1, n_phi)
    has_before, has_after = phi > 0, phi < n_phi - 1
    own_tilts, own_phis = frames_ref.shape[:2]
    blocks, all_tilts, phis = data_ref.shape[:3]
    sizes = (HALO, HALO, own_tilts - 2 * HALO)
    firsts = (0, own_tilts - HALO, HALO)

    band_load = pltpu.make_async_copy(band_hbm, band_ref, band_sem)
    band_load.start()
    loads = []
    for number, (first, size) in enumerate(zip(firsts, sizes)):
        part = pl.ds(first, size)
        loads.append(pltpu.make_async_copy(frames_hbm.at[part], frames_ref.at[part], frame_sems.at[number]))
        loads[-1].start()

    barrier = pltpu.get_barrier_semaphore()
    peers = [(before, 0), (before, 1), (after, 0), (after, 1)]

    def greet(to_phi, to_chi):
        pl.semaphore_signal(
            barrier, inc=1, device_id={"chi": to_chi, "phi": to_phi}, device_id_type=pl.DeviceIdType.MESH
        )

    def with_neighbours(act):
        @pl.when(has_before)
        def _():
            for number in (0, 1):
                act(number)

        @pl.when(has_after)
        def _():
            for number in (2, 3):
                act(number)

    with_neighbours(lambda number: greet(*peers[number]))
    greet(phi, other)

    empty = jnp.zeros(spread_ref.shape[2:], jnp.float32)
    for p in range(own_phis):
        for r in range(PAD_ROWS):
            spread_ref[p, r] = empty
            spread_ref[p, spread_ref.shape[1] - 1 - r] = empty

    def shift_tilts(first, size):
        def step(tilt, carry):
            shift_tilt(tilt, rows_ref, cols_ref, index_ref, frames_ref, spread_ref, staged_ref)
            return carry

        lax.fori_loop(first, first + size, step, 0)

    mine = pl.ds(chi * own_phis, own_phis)

    def neighbour_copy(b, number):
        to_phi, to_chi = peers[number]
        back = number < 2
        from_tilts = pl.ds(0 if back else own_tilts - HALO, HALO)
        to_tilts = pl.ds(all_tilts - HALO if back else 0, HALO)
        place = (0 if back else 2) + chi
        return pltpu.make_async_remote_copy(
            src_ref=staged_ref.at[to_chi, b, from_tilts],
            dst_ref=data_ref.at[b, to_tilts, mine],
            send_sem=send_sems.at[b, number],
            recv_sem=recv_sems.at[b, place],
            device_id={"chi": to_chi, "phi": to_phi},
            device_id_type=pl.DeviceIdType.MESH,
        )

    def arrival(b, place):
        back = place < 2
        to_tilts = pl.ds(all_tilts - HALO if back else 0, HALO)
        from_chi = place % 2
        return pltpu.make_async_remote_copy(
            src_ref=staged_ref.at[0, b, pl.ds(0, HALO)],
            dst_ref=data_ref.at[b, to_tilts, pl.ds(from_chi * own_phis, own_phis)],
            send_sem=send_sems.at[b, place],
            recv_sem=recv_sems.at[b, place],
            device_id={"chi": from_chi, "phi": after if back else before},
            device_id_type=pl.DeviceIdType.MESH,
        )

    middle = pl.ds(HALO, own_tilts)

    def pair_copy(b, phis_at):
        return pltpu.make_async_remote_copy(
            src_ref=staged_ref.at[other, b],
            dst_ref=data_ref.at[b, middle, phis_at],
            send_sem=pair_sends.at[b],
            recv_sem=pair_recvs.at[b],
            device_id={"chi": other, "phi": phi},
            device_id_type=pl.DeviceIdType.MESH,
        )

    def local_copy(b):
        return pltpu.make_async_copy(staged_ref.at[chi, b], data_ref.at[b, middle, mine], local_sems.at[b])

    loads[0].wait()
    shift_tilts(firsts[0], sizes[0])
    loads[1].wait()
    shift_tilts(firsts[1], sizes[1])
    pl.semaphore_wait(barrier, 1 + 2 * has_before.astype(jnp.int32) + 2 * has_after.astype(jnp.int32))

    def send_halos(b, carry):
        with_neighbours(lambda number: neighbour_copy(b, number).start())
        return carry

    lax.fori_loop(0, blocks, send_halos, 0)
    loads[2].wait()
    shift_tilts(firsts[2], sizes[2])

    def send_pairs(b, carry):
        pair_copy(b, mine).start()
        local_copy(b).start()
        return carry

    lax.fori_loop(0, blocks, send_pairs, 0)
    band_load.wait()

    left_add = jnp.where(phi == 0, 0.0, 0.1)
    right_add = jnp.where(phi == n_phi - 1, 0.0, 0.1)

    def block(b, carry):
        pair_copy(b, pl.ds(other * own_phis, own_phis)).wait_recv()
        local_copy(b).wait()
        nothing = jnp.zeros(data_ref.shape[2:], jnp.float32)

        @pl.when(has_before)
        def _():
            for place in (2, 3):
                arrival(b, place).wait_recv()

        @pl.when(phi == 0)
        def _():
            for c in range(HALO):
                data_ref[b, c] = nothing

        @pl.when(has_after)
        def _():
            for place in (0, 1):
                arrival(b, place).wait_recv()

        @pl.when(phi == n_phi - 1)
        def _():
            for c in range(all_tilts - HALO, all_tilts):
                data_ref[b, c] = nothing

        even, odd = tap_matrices(band_ref[pl.ds(pl.multiple_of(b * SUBS, SUBS), SUBS), :])

        def start(c):
            add = jnp.where(c < HALO, left_add, jnp.where(c >= HALO + own_tilts, right_add, 0.1))
            return [data_ref[b, c, p] + add for p in range(phis)]

        def held(c):
            return [estimate_ref[c, p] for p in range(phis)]

        def ratios(c):
            return [ratio_ref[c, p] for p in range(phis)]

        for iteration in range(ITERS):
            estimate = start if iteration == 0 else held
            margin = 2 * iteration + 1

            def to_ratio(c, blurred):
                for p in range(phis):
                    ratio_ref[c, p] = data_ref[b, c, p] / (blurred[p] + 0.1)

            def to_estimate(c, factor):
                made = [a * f for a, f in zip(estimate(c), factor)]
                if iteration < ITERS - 1:
                    for p in range(phis):
                        estimate_ref[c, p] = made[p]
                else:
                    planes = pl.ds(pl.multiple_of(b * SUBS, SUBS), SUBS)
                    out_ref[c - HALO, planes] = jnp.swapaxes(jnp.stack(made), 0, 1)

            sweep(estimate, to_ratio, margin, all_tilts - margin, even, odd)
            sweep(ratios, to_estimate, margin + 1, all_tilts - margin - 1, even, odd)
        return carry

    lax.fori_loop(0, blocks, block, 0)

    def finish(b, carry):
        with_neighbours(lambda number: neighbour_copy(b, number).wait_send())
        pair_copy(b, mine).wait_send()
        return carry

    lax.fori_loop(0, blocks, finish, 0)


def body(n_phi, frames, drift_rows, drift_cols, weight_index, blur_band):
    tilts, own_phis, rows, cols = frames.shape
    pixels = blur_band.shape[0]
    phis = 2 * own_phis
    planes = pixels // LANES
    blocks = planes // SUBS
    tile = (SUBS, LANES)
    all_tilts = tilts + 2 * HALO
    hbm = pl.BlockSpec(memory_space=pltpu.HBM)
    smem = pl.BlockSpec(memory_space=pltpu.SMEM)
    out = pl.pallas_call(
        functools.partial(kernel, n_phi),
        out_shape=pltpu.VMEM((tilts, planes, phis, LANES), jnp.float32),
        in_specs=[smem] * 3 + [hbm] * 2,
        out_specs=pl.BlockSpec(memory_space=pltpu.VMEM),
        scratch_shapes=[
            pltpu.VMEM((planes, LANES), jnp.int32),
            pltpu.VMEM(frames.shape, frames.dtype),
            pltpu.VMEM((own_phis, rows + 2 * PAD_ROWS, cols // LANES // SUBS) + tile, jnp.float32),
            pltpu.VMEM((2, blocks, tilts, own_phis) + tile, jnp.float32),
            pltpu.VMEM((blocks, all_tilts, phis) + tile, jnp.float32),
            pltpu.VMEM((all_tilts, phis) + tile, jnp.float32),
            pltpu.VMEM((all_tilts, phis) + tile, jnp.float32),
            pltpu.SemaphoreType.DMA,
            pltpu.SemaphoreType.DMA((3,)),
            pltpu.SemaphoreType.DMA((blocks, REMOTE)),
            pltpu.SemaphoreType.DMA((blocks, REMOTE)),
            pltpu.SemaphoreType.DMA((blocks,)),
            pltpu.SemaphoreType.DMA((blocks,)),
            pltpu.SemaphoreType.DMA((blocks,)),
        ],
        compiler_params=pltpu.CompilerParams(
            collective_id=0, has_side_effects=True, vmem_limit_bytes=56 * 1024 * 1024
        ),
        name="rocking",
    )(drift_rows.T, drift_cols.T, weight_index.T, blur_band.reshape(planes, LANES), frames)
    return out.transpose(0, 2, 1, 3).reshape(tilts, phis, pixels)


def solution(mesh):
    return jax.shard_map(
        functools.partial(body, mesh.shape["phi"]),
        mesh=mesh,
        in_specs=(
            P("phi", "chi", None, None),
            P("phi", "chi"),
            P("phi", "chi"),
            P("phi", "chi"),
            P("chi"),
        ),
        out_specs=P("phi", None, "chi"),
        check_vma=False,
    )
```

```python
import functools

import jax
import jax.numpy as jnp
from jax import lax
from jax.experimental import pallas as pl
from jax.experimental.pallas import tpu as pltpu
from jax.sharding import PartitionSpec as P

ITERS = 3
HALO = 2 * ITERS
LANES = 128
SUBS = 8
MOST_ROWS = 2
PAD_ROWS = MOST_ROWS + 1
REMOTE = 4


def shift_tilt(tilt, rows_ref, cols_ref, index_ref, frames_ref, spread_ref, staged_ref):
    own_phis, rows, cols = frames_ref.shape[1:]
    tiles = cols // LANES
    halves = tiles // SUBS
    blocks = staged_ref.shape[1]
    lane = lax.broadcasted_iota(jnp.int32, (rows, LANES), 1)
    zero = jnp.zeros((rows, LANES), jnp.float32)
    for p in range(own_phis):
        drift_col = cols_ref[p, tilt]
        frac_x = (index_ref[p, tilt] & 7).astype(jnp.float32) / 8.0
        turn = (drift_col + LANES) & (LANES - 1)
        from_left = lane < drift_col
        from_right = lane >= LANES + drift_col
        frame = frames_ref[tilt, p].astype(jnp.float32)
        source = [frame[:, t * LANES : (t + 1) * LANES] for t in range(tiles)] + [zero]
        stepped = [pltpu.roll(s, 1, 1) for s in source[:-1]]
        turned = []
        for t in range(tiles + 1):
            before = stepped[t - 1] if t > 0 else zero
            here = stepped[t] if t < tiles else zero
            mixed = (1.0 - frac_x) * source[t] + frac_x * jnp.where(lane < 1, before, here)
            turned.append(pltpu.roll(mixed, turn, 1))
        moved = []
        for t in range(tiles):
            left = turned[t - 1] if t > 0 else zero
            moved.append(jnp.where(from_left, left, jnp.where(from_right, turned[t + 1], turned[t])))
        for h in range(halves):
            group = jnp.stack(moved[h * SUBS : (h + 1) * SUBS])
            spread_ref[p, PAD_ROWS : PAD_ROWS + rows, h] = jnp.swapaxes(group, 0, 1)
    for p in range(own_phis):
        drift_row = rows_ref[p, tilt]
        frac_y = (index_ref[p, tilt] >> 3).astype(jnp.float32) / 8.0
        for r in range(rows):
            row = (1.0 - frac_y) * spread_ref[p, r + PAD_ROWS - drift_row] + frac_y * spread_ref[
                p, r + PAD_ROWS - 1 - drift_row
            ]
            for h in range(halves):
                place = r * halves + h
                staged_ref[place // blocks, place % blocks, tilt, p] = row[h]


def tap_matrices(band):
    spread = 0.8 + 0.6 * band.astype(jnp.float32)
    unnormed = [jnp.exp(-float(k * k) / (2.0 * spread * spread)) for k in range(5)]
    total = unnormed[0] + 2.0 * (unnormed[1] + unnormed[2] + unnormed[3] + unnormed[4])
    taps = [0.125 * (u / total) for u in unnormed]
    made = {}

    def pair(near, far, sign):
        if far > 4:
            return taps[near]
        if (near, far, sign) not in made:
            made[near, far, sign] = taps[near] + sign * taps[far] if near < far else taps[near] * 1.0 + sign * taps[far]
        return made[near, far, sign]

    even = [[pair(abs(p - q), 7 - p - q, 1.0) for q in range(4)] for p in range(4)]
    odd = [[pair(abs(p - q), 7 - p - q, -1.0) for q in range(4)] for p in range(4)]
    return even, odd


def phi_blur(tilts, even, odd):
    plus = [tilts[p] + tilts[7 - p] for p in range(4)]
    minus = [tilts[p] - tilts[7 - p] for p in range(4)]
    halves = []
    for matrix, parts in ((even, plus), (odd, minus)):
        rows = []
        for p in range(4):
            row = matrix[p][0] * parts[0]
            for q in range(1, 4):
                row = row + matrix[p][q] * parts[q]
            rows.append(row)
        halves.append(rows)
    front = [halves[0][p] + halves[1][p] for p in range(4)]
    back = [halves[0][3 - p] - halves[1][3 - p] for p in range(4)]
    return front + back


def kernel(
    n_phi,
    rows_ref,
    cols_ref,
    index_ref,
    band_hbm,
    frames_hbm,
    out_ref,
    band_ref,
    frames_ref,
    spread_ref,
    staged_ref,
    data_ref,
    estimate_ref,
    blurs_ref,
    band_sem,
    frame_sems,
    send_sems,
    recv_sems,
    last_sends,
    last_recvs,
    pair_sends,
    pair_recvs,
    local_sems,
):
    chi, phi = lax.axis_index("chi"), lax.axis_index("phi")
    other = 1 - chi
    before = lax.rem(phi + n_phi - 1, n_phi)
    after = lax.rem(phi + 1, n_phi)
    has_before, has_after = phi > 0, phi < n_phi - 1
    own_tilts, own_phis = frames_ref.shape[:2]
    blocks, all_tilts, phis = data_ref.shape[:3]
    sizes = (HALO, HALO, own_tilts - 2 * HALO)
    firsts = (0, own_tilts - HALO, HALO)

    band_load = pltpu.make_async_copy(band_hbm, band_ref, band_sem)
    band_load.start()
    loads = []
    for number, (first, size) in enumerate(zip(firsts, sizes)):
        part = pl.ds(first, size)
        loads.append(pltpu.make_async_copy(frames_hbm.at[part], frames_ref.at[part], frame_sems.at[number]))
        loads[-1].start()

    barrier = pltpu.get_barrier_semaphore()
    peers = [(before, 0), (before, 1), (after, 0), (after, 1)]

    def greet(to_phi, to_chi):
        pl.semaphore_signal(
            barrier, inc=1, device_id={"chi": to_chi, "phi": to_phi}, device_id_type=pl.DeviceIdType.MESH
        )

    def with_neighbours(act):
        @pl.when(has_before)
        def _():
            for number in (0, 1):
                act(number)

        @pl.when(has_after)
        def _():
            for number in (2, 3):
                act(number)

    with_neighbours(lambda number: greet(*peers[number]))
    greet(phi, other)

    empty = jnp.zeros(spread_ref.shape[2:], jnp.float32)
    for p in range(own_phis):
        for r in range(PAD_ROWS):
            spread_ref[p, r] = empty
            spread_ref[p, spread_ref.shape[1] - 1 - r] = empty

    def shift_tilts(first, size):
        def step(tilt, carry):
            shift_tilt(tilt, rows_ref, cols_ref, index_ref, frames_ref, spread_ref, staged_ref)
            return carry

        lax.fori_loop(first, first + size, step, 0)

    mine = pl.ds(chi * own_phis, own_phis)

    def neighbour_copy(b, number, tilt, tilts, send_sem, recv_sem, flip):
        back = number < 2
        to_chi = lax.rem(flip + number, 2)
        first = 0 if back else own_tilts - HALO
        first_there = all_tilts - HALO if back else 0
        return pltpu.make_async_remote_copy(
            src_ref=staged_ref.at[to_chi, b, pl.ds(first + tilt, tilts)],
            dst_ref=data_ref.at[b, pl.ds(first_there + tilt, tilts), mine],
            send_sem=send_sem,
            recv_sem=recv_sem,
            device_id={"chi": to_chi, "phi": before if back else after},
            device_id_type=pl.DeviceIdType.MESH,
        )

    def place_of(number):
        return (0 if number < 2 else 2) + chi

    def halo_copy(b, number, tilt=0, tilts=HALO):
        return neighbour_copy(b, number, tilt, tilts, send_sems.at[b, number], recv_sems.at[b, place_of(number)], b)

    def last_copy(number, step):
        tilt = step if number < 2 else HALO - 1 - step
        return neighbour_copy(
            blocks - 1, number, tilt, 1, last_sends.at[number, step], last_recvs.at[place_of(number), step], step
        )

    def arrival(b, place, tilt, tilts, recv_sem):
        back = place < 2
        from_chi = place % 2
        first = all_tilts - HALO if back else 0
        return pltpu.make_async_remote_copy(
            src_ref=staged_ref.at[0, b, pl.ds(0, tilts)],
            dst_ref=data_ref.at[b, pl.ds(first + tilt, tilts), pl.ds(from_chi * own_phis, own_phis)],
            send_sem=send_sems.at[0, place],
            recv_sem=recv_sem,
            device_id={"chi": from_chi, "phi": after if back else before},
            device_id_type=pl.DeviceIdType.MESH,
        )

    middle = pl.ds(HALO, own_tilts)

    def pair_copy(b, phis_at):
        return pltpu.make_async_remote_copy(
            src_ref=staged_ref.at[other, b],
            dst_ref=data_ref.at[b, middle, phis_at],
            send_sem=pair_sends.at[b],
            recv_sem=pair_recvs.at[b],
            device_id={"chi": other, "phi": phi},
            device_id_type=pl.DeviceIdType.MESH,
        )

    def local_copy(b):
        return pltpu.make_async_copy(staged_ref.at[chi, b], data_ref.at[b, middle, mine], local_sems.at[b])

    loads[0].wait()
    loads[1].wait()
    pl.semaphore_wait(barrier, 1 + 2 * has_before.astype(jnp.int32) + 2 * has_after.astype(jnp.int32))

    def shift_edges(tilt, carry):
        for first in firsts[:2]:
            shift_tilt(first + tilt, rows_ref, cols_ref, index_ref, frames_ref, spread_ref, staged_ref)
        with_neighbours(lambda number: halo_copy(0, number, tilt, 1).start())
        return carry

    lax.fori_loop(0, HALO, shift_edges, 0)

    def send_halos(b, carry):
        with_neighbours(lambda number: halo_copy(b, number).start())
        return carry

    lax.fori_loop(1, blocks - 1, send_halos, 0)

    def send_last(step, carry):
        with_neighbours(lambda number: last_copy(number, step).start())
        return carry

    lax.fori_loop(0, HALO, send_last, 0)
    loads[2].wait()
    shift_tilts(firsts[2], sizes[2])

    def send_pairs(b, carry):
        pair_copy(b, mine).start()
        local_copy(b).start()
        return carry

    lax.fori_loop(0, blocks, send_pairs, 0)
    band_load.wait()

    left_add = jnp.where(phi == 0, 0.0, 0.1)
    right_add = jnp.where(phi == n_phi - 1, 0.0, 0.1)

    def block(b, last):
        even, odd = tap_matrices(band_ref[pl.ds(pl.multiple_of(b * SUBS, SUBS), SUBS), :])
        stages = 2 * ITERS

        def blurs(stage, c):
            return [blurs_ref[stage, c, p] for p in range(phis)]

        def keep_blur(stage, c, values):
            made = phi_blur(values, even, odd)
            for p in range(phis):
                blurs_ref[stage, c, p] = made[p]
            return made

        def first_estimate(c, add):
            return [data_ref[b, c, p] + add for p in range(phis)]

        def finish_cell(stage, c, mixed, add):
            if stage % 2 == 1:
                made = [data_ref[b, c, p] / (mixed[p] + 0.1) for p in range(phis)]
            else:
                old = first_estimate(c, add) if stage == 2 else [estimate_ref[c, p] for p in range(phis)]
                made = [o * m for o, m in zip(old, mixed)]
                if stage < stages:
                    for p in range(phis):
                        estimate_ref[c, p] = made[p]
            if stage < stages:
                return keep_blur(stage, c, made)
            planes = pl.ds(pl.multiple_of(b * SUBS, SUBS), SUBS)
            out_ref[c - HALO, planes] = jnp.swapaxes(jnp.stack(made), 0, 1)
            return made

        pair_copy(b, pl.ds(other * own_phis, own_phis)).wait_recv()
        local_copy(b).wait()

        def start_cell(c, carry):
            keep_blur(0, c, first_estimate(c, 0.1))
            return carry

        lax.fori_loop(HALO, HALO + own_tilts, start_cell, 0, unroll=2)
        for stage in range(1, stages + 1):
            low, high = HALO + stage, HALO + own_tilts - stage

            def cell(c, carry):
                here, joined = carry
                beyond = blurs(stage - 1, c + 1)
                ahead = [x + y for x, y in zip(here, beyond)]
                finish_cell(stage, c, [x + y for x, y in zip(joined, ahead)], 0.1)
                return beyond, ahead

            near, here = blurs(stage - 1, low - 1), blurs(stage - 1, low)
            lax.fori_loop(low, high, cell, (here, [x + y for x, y in zip(near, here)]), unroll=2)

        nothing = jnp.zeros(data_ref.shape[2:], jnp.float32)

        @pl.when(phi == 0)
        def _():
            for c in range(HALO):
                data_ref[b, c] = nothing

        @pl.when(phi == n_phi - 1)
        def _():
            for c in range(all_tilts - HALO, all_tilts):
                data_ref[b, c] = nothing

        def wait_for(places, back_tilt, step):
            for place in places:
                if last:
                    arrival(b, place, back_tilt, 1, last_recvs.at[place, step]).wait_recv()
                else:
                    arrival(b, place, 0, HALO, recv_sems.at[b, place]).wait_recv()

        def wait_step(step):
            @pl.when(has_before)
            def _():
                wait_for((2, 3), HALO - 1 - step, step)

            @pl.when(has_after)
            def _():
                wait_for((0, 1), step, step)

        if not last:
            wait_step(0)

        def wave(step, carry):
            if last:
                wait_step(step)
            tilts = (HALO - 1 - step, HALO + own_tilts + step)
            steps = (1, -1)
            adds = (left_add, right_add)
            chain = [keep_blur(0, c, first_estimate(c, add)) for c, add in zip(tilts, adds)]
            for stage in range(1, stages + 1):
                for side in range(2):
                    c = tilts[side] + steps[side] * stage
                    here, beyond = blurs(stage - 1, c), blurs(stage - 1, c + steps[side])
                    mixed = [(x + y) + (y + z) for x, y, z in zip(chain[side], here, beyond)]
                    outside = c < HALO if side == 0 else c >= HALO + own_tilts
                    chain[side] = finish_cell(stage, c, mixed, jnp.where(outside, adds[side], 0.1))
            return carry

        lax.fori_loop(0, HALO, wave, 0)

    def some_block(b, carry):
        block(b, False)
        return carry

    lax.fori_loop(0, blocks - 1, some_block, 0)
    block(blocks - 1, True)

    def finish(b, carry):
        with_neighbours(lambda number: halo_copy(b, number).wait_send())
        return carry

    lax.fori_loop(0, blocks - 1, finish, 0)

    def finish_last(step, carry):
        with_neighbours(lambda number: last_copy(number, step).wait_send())
        return carry

    lax.fori_loop(0, HALO, finish_last, 0)

    def finish_pair(b, carry):
        pair_copy(b, mine).wait_send()
        return carry

    lax.fori_loop(0, blocks, finish_pair, 0)


def body(n_phi, frames, drift_rows, drift_cols, weight_index, blur_band):
    tilts, own_phis, rows, cols = frames.shape
    pixels = blur_band.shape[0]
    phis = 2 * own_phis
    planes = pixels // LANES
    blocks = planes // SUBS
    tile = (SUBS, LANES)
    all_tilts = tilts + 2 * HALO
    hbm = pl.BlockSpec(memory_space=pltpu.HBM)
    smem = pl.BlockSpec(memory_space=pltpu.SMEM)
    out = pl.pallas_call(
        functools.partial(kernel, n_phi),
        out_shape=pltpu.VMEM((tilts, planes, phis, LANES), jnp.float32),
        in_specs=[smem] * 3 + [hbm] * 2,
        out_specs=pl.BlockSpec(memory_space=pltpu.VMEM),
        scratch_shapes=[
            pltpu.VMEM((planes, LANES), jnp.int32),
            pltpu.VMEM(frames.shape, frames.dtype),
            pltpu.VMEM((own_phis, rows + 2 * PAD_ROWS, cols // LANES // SUBS) + tile, jnp.float32),
            pltpu.VMEM((2, blocks, tilts, own_phis) + tile, jnp.float32),
            pltpu.VMEM((blocks, all_tilts, phis) + tile, jnp.float32),
            pltpu.VMEM((all_tilts, phis) + tile, jnp.float32),
            pltpu.VMEM((2 * ITERS, all_tilts, phis) + tile, jnp.float32),
            pltpu.SemaphoreType.DMA,
            pltpu.SemaphoreType.DMA((3,)),
            pltpu.SemaphoreType.DMA((blocks - 1, REMOTE)),
            pltpu.SemaphoreType.DMA((blocks - 1, REMOTE)),
            pltpu.SemaphoreType.DMA((REMOTE, HALO)),
            pltpu.SemaphoreType.DMA((REMOTE, HALO)),
            pltpu.SemaphoreType.DMA((blocks,)),
            pltpu.SemaphoreType.DMA((blocks,)),
            pltpu.SemaphoreType.DMA((blocks,)),
        ],
        compiler_params=pltpu.CompilerParams(
            collective_id=0, has_side_effects=True, vmem_limit_bytes=56 * 1024 * 1024
        ),
        name="rocking",
    )(drift_rows.T, drift_cols.T, weight_index.T, blur_band.reshape(planes, LANES), frames)
    return out.transpose(0, 2, 1, 3).reshape(tilts, phis, pixels)


def solution(mesh):
    return jax.shard_map(
        functools.partial(body, mesh.shape["phi"]),
        mesh=mesh,
        in_specs=(
            P("phi", "chi", None, None),
            P("phi", "chi"),
            P("phi", "chi"),
            P("phi", "chi"),
            P("chi"),
        ),
        out_specs=P("phi", None, "chi"),
        check_vma=False,
    )
```

```python
import functools

import jax
import jax.numpy as jnp
from jax import lax
from jax.experimental import pallas as pl
from jax.experimental.pallas import tpu as pltpu
from jax.sharding import PartitionSpec as P

ITERS = 3
HALO = 2 * ITERS
LANES = 128
SUBS = 8
MOST_ROWS = 2
PAD_ROWS = MOST_ROWS + 1
REMOTE = 4


def shift_tilt(tilt, rows_ref, cols_ref, index_ref, frames_ref, spread_ref, staged_ref):
    own_phis, rows, cols = frames_ref.shape[1:]
    tiles = cols // LANES
    halves = tiles // SUBS
    blocks = staged_ref.shape[1]
    lane = lax.broadcasted_iota(jnp.int32, (rows, LANES), 1)
    zero = jnp.zeros((rows, LANES), jnp.float32)
    for p in range(own_phis):
        drift_col = cols_ref[p, tilt]
        frac_x = (index_ref[p, tilt] & 7).astype(jnp.float32) / 8.0
        turn = (drift_col + LANES) & (LANES - 1)
        from_left = lane < drift_col
        from_right = lane >= LANES + drift_col
        frame = frames_ref[tilt, p].astype(jnp.float32)
        source = [frame[:, t * LANES : (t + 1) * LANES] for t in range(tiles)] + [zero]
        stepped = [pltpu.roll(s, 1, 1) for s in source[:-1]]
        turned = []
        for t in range(tiles + 1):
            before = stepped[t - 1] if t > 0 else zero
            here = stepped[t] if t < tiles else zero
            mixed = (1.0 - frac_x) * source[t] + frac_x * jnp.where(lane < 1, before, here)
            turned.append(pltpu.roll(mixed, turn, 1))
        moved = []
        for t in range(tiles):
            left = turned[t - 1] if t > 0 else zero
            moved.append(jnp.where(from_left, left, jnp.where(from_right, turned[t + 1], turned[t])))
        for h in range(halves):
            group = jnp.stack(moved[h * SUBS : (h + 1) * SUBS])
            spread_ref[p, PAD_ROWS : PAD_ROWS + rows, h] = jnp.swapaxes(group, 0, 1)
    for p in range(own_phis):
        drift_row = jnp.clip(rows_ref[p, tilt], -MOST_ROWS, MOST_ROWS)
        frac_y = (index_ref[p, tilt] >> 3).astype(jnp.float32) / 8.0
        for r in range(rows):
            row = (1.0 - frac_y) * spread_ref[p, r + PAD_ROWS - drift_row] + frac_y * spread_ref[
                p, r + PAD_ROWS - 1 - drift_row
            ]
            for h in range(halves):
                place = r * halves + h
                staged_ref[place // blocks, place % blocks, tilt, p] = row[h]


def tap_matrices(band):
    spread = 0.8 + 0.6 * band.astype(jnp.float32)
    unnormed = [jnp.exp(-float(k * k) / (2.0 * spread * spread)) for k in range(5)]
    total = unnormed[0] + 2.0 * (unnormed[1] + unnormed[2] + unnormed[3] + unnormed[4])
    taps = [0.125 * (u / total) for u in unnormed]
    made = {}

    def pair(near, far, sign):
        if far > 4:
            return taps[near]
        if (near, far, sign) not in made:
            made[near, far, sign] = taps[near] + sign * taps[far] if near < far else taps[near] * 1.0 + sign * taps[far]
        return made[near, far, sign]

    even = [[pair(abs(p - q), 7 - p - q, 1.0) for q in range(4)] for p in range(4)]
    odd = [[pair(abs(p - q), 7 - p - q, -1.0) for q in range(4)] for p in range(4)]
    return even, odd


def phi_blur(tilts, even, odd):
    plus = [tilts[p] + tilts[7 - p] for p in range(4)]
    minus = [tilts[p] - tilts[7 - p] for p in range(4)]
    halves = []
    for matrix, parts in ((even, plus), (odd, minus)):
        rows = []
        for p in range(4):
            row = matrix[p][0] * parts[0]
            for q in range(1, 4):
                row = row + matrix[p][q] * parts[q]
            rows.append(row)
        halves.append(rows)
    front = [halves[0][p] + halves[1][p] for p in range(4)]
    back = [halves[0][3 - p] - halves[1][3 - p] for p in range(4)]
    return front + back


def kernel(
    n_phi,
    rows_hbm,
    cols_hbm,
    index_hbm,
    band_hbm,
    frames_hbm,
    out_ref,
    rows_ref,
    cols_ref,
    index_ref,
    band_ref,
    frames_ref,
    spread_ref,
    staged_ref,
    data_ref,
    estimate_ref,
    blurs_ref,
    table_sems,
    band_sem,
    edge_sems,
    middle_sem,
    send_sems,
    recv_sems,
    last_sends,
    last_recvs,
    pair_sends,
    pair_recvs,
    local_sems,
):
    chi, phi = lax.axis_index("chi"), lax.axis_index("phi")
    other = 1 - chi
    before = lax.rem(phi + n_phi - 1, n_phi)
    after = lax.rem(phi + 1, n_phi)
    has_before, has_after = phi > 0, phi < n_phi - 1
    own_tilts, own_phis = frames_ref.shape[:2]
    blocks, all_tilts, phis = data_ref.shape[:3]
    firsts = (0, own_tilts - HALO)

    def edge_load(tilt, side):
        at = firsts[side] + tilt
        return pltpu.make_async_copy(frames_hbm.at[at], frames_ref.at[at], edge_sems.at[tilt, side])

    tables = ((rows_hbm, rows_ref), (cols_hbm, cols_ref), (index_hbm, index_ref))
    table_loads = [pltpu.make_async_copy(a, b, table_sems.at[i]) for i, (a, b) in enumerate(tables)]
    for load in table_loads:
        load.start()
    for tilt in range(HALO):
        for side in range(2):
            edge_load(tilt, side).start()
    inner = pl.ds(HALO, own_tilts - 2 * HALO)
    middle_load = pltpu.make_async_copy(frames_hbm.at[inner], frames_ref.at[inner], middle_sem)
    middle_load.start()
    band_load = pltpu.make_async_copy(band_hbm, band_ref, band_sem)
    band_load.start()

    barrier = pltpu.get_barrier_semaphore()
    peers = [(before, 0), (before, 1), (after, 0), (after, 1)]

    def greet(to_phi, to_chi):
        pl.semaphore_signal(
            barrier, inc=1, device_id={"chi": to_chi, "phi": to_phi}, device_id_type=pl.DeviceIdType.MESH
        )

    def with_neighbours(act):
        @pl.when(has_before)
        def _():
            for number in (0, 1):
                act(number)

        @pl.when(has_after)
        def _():
            for number in (2, 3):
                act(number)

    with_neighbours(lambda number: greet(*peers[number]))
    greet(phi, other)

    empty = jnp.zeros(spread_ref.shape[2:], jnp.float32)
    for p in range(own_phis):
        for r in range(PAD_ROWS):
            spread_ref[p, r] = empty
            spread_ref[p, spread_ref.shape[1] - 1 - r] = empty

    mine = pl.ds(chi * own_phis, own_phis)

    def neighbour_copy(b, number, tilt, tilts, send_sem, recv_sem, flip):
        back = number < 2
        to_chi = lax.rem(flip + number, 2)
        first = 0 if back else own_tilts - HALO
        first_there = all_tilts - HALO if back else 0
        return pltpu.make_async_remote_copy(
            src_ref=staged_ref.at[to_chi, b, pl.ds(first + tilt, tilts)],
            dst_ref=data_ref.at[b, pl.ds(first_there + tilt, tilts), mine],
            send_sem=send_sem,
            recv_sem=recv_sem,
            device_id={"chi": to_chi, "phi": before if back else after},
            device_id_type=pl.DeviceIdType.MESH,
        )

    def place_of(number):
        return (0 if number < 2 else 2) + chi

    def halo_copy(b, number, tilt=0, tilts=HALO):
        return neighbour_copy(b, number, tilt, tilts, send_sems.at[b, number], recv_sems.at[b, place_of(number)], b)

    def last_copy(number, step):
        tilt = step if number < 2 else HALO - 1 - step
        return neighbour_copy(
            blocks - 1, number, tilt, 1, last_sends.at[number, step], last_recvs.at[place_of(number), step], step
        )

    def arrival(b, place, tilt, tilts, recv_sem):
        back = place < 2
        from_chi = place % 2
        first = all_tilts - HALO if back else 0
        return pltpu.make_async_remote_copy(
            src_ref=staged_ref.at[0, b, pl.ds(0, tilts)],
            dst_ref=data_ref.at[b, pl.ds(first + tilt, tilts), pl.ds(from_chi * own_phis, own_phis)],
            send_sem=send_sems.at[0, place],
            recv_sem=recv_sem,
            device_id={"chi": from_chi, "phi": after if back else before},
            device_id_type=pl.DeviceIdType.MESH,
        )

    middle = pl.ds(HALO, own_tilts)

    def pair_copy(b, phis_at):
        return pltpu.make_async_remote_copy(
            src_ref=staged_ref.at[other, b],
            dst_ref=data_ref.at[b, middle, phis_at],
            send_sem=pair_sends.at[b],
            recv_sem=pair_recvs.at[b],
            device_id={"chi": other, "phi": phi},
            device_id_type=pl.DeviceIdType.MESH,
        )

    def local_copy(b):
        return pltpu.make_async_copy(staged_ref.at[chi, b], data_ref.at[b, middle, mine], local_sems.at[b])

    def shift_at(tilt):
        shift_tilt(tilt, rows_ref, cols_ref, index_ref, frames_ref, spread_ref, staged_ref)

    for load in table_loads:
        load.wait()

    def shift_edges(tilt, carry):
        for side in range(2):
            edge_load(tilt, side).wait()
            shift_at(firsts[side] + tilt)

        @pl.when(tilt == 0)
        def _():
            pl.semaphore_wait(barrier, 1 + 2 * has_before.astype(jnp.int32) + 2 * has_after.astype(jnp.int32))

        with_neighbours(lambda number: halo_copy(0, number, tilt, 1).start())
        return carry

    lax.fori_loop(0, HALO, shift_edges, 0)

    def send_halos(b, carry):
        with_neighbours(lambda number: halo_copy(b, number).start())
        return carry

    lax.fori_loop(1, blocks - 1, send_halos, 0)

    def send_last(step, carry):
        with_neighbours(lambda number: last_copy(number, step).start())
        return carry

    lax.fori_loop(0, HALO, send_last, 0)
    middle_load.wait()

    def shift_inner(tilt, carry):
        shift_at(tilt)
        return carry

    lax.fori_loop(HALO, own_tilts - HALO, shift_inner, 0)

    def send_pairs(b, carry):
        pair_copy(b, mine).start()
        local_copy(b).start()
        return carry

    lax.fori_loop(0, blocks, send_pairs, 0)
    band_load.wait()

    left_add = jnp.where(phi == 0, 0.0, 0.1)
    right_add = jnp.where(phi == n_phi - 1, 0.0, 0.1)

    def block(b, last):
        even, odd = tap_matrices(band_ref[pl.ds(pl.multiple_of(b * SUBS, SUBS), SUBS), :])
        stages = 2 * ITERS

        def blurs(stage, c):
            return [blurs_ref[stage, c, p] for p in range(phis)]

        def keep_blur(stage, c, values):
            made = phi_blur(values, even, odd)
            for p in range(phis):
                blurs_ref[stage, c, p] = made[p]
            return made

        def first_estimate(c, add):
            return [data_ref[b, c, p] + add for p in range(phis)]

        def finish_cell(stage, c, mixed, add):
            if stage % 2 == 1:
                made = [data_ref[b, c, p] / (mixed[p] + 0.1) for p in range(phis)]
            else:
                old = first_estimate(c, add) if stage == 2 else [estimate_ref[c, p] for p in range(phis)]
                made = [o * m for o, m in zip(old, mixed)]
                if stage < stages:
                    for p in range(phis):
                        estimate_ref[c, p] = made[p]
            if stage < stages:
                return keep_blur(stage, c, made)
            planes = pl.ds(pl.multiple_of(b * SUBS, SUBS), SUBS)
            out_ref[c - HALO, planes] = jnp.swapaxes(jnp.stack(made), 0, 1)
            return made

        pair_copy(b, pl.ds(other * own_phis, own_phis)).wait_recv()
        local_copy(b).wait()

        def start_cell(c, carry):
            keep_blur(0, c, first_estimate(c, 0.1))
            return carry

        lax.fori_loop(HALO, HALO + own_tilts, start_cell, 0, unroll=2)
        for stage in range(1, stages + 1):
            low, high = HALO + stage, HALO + own_tilts - stage

            def cell(c, carry):
                here, joined = carry
                beyond = blurs(stage - 1, c + 1)
                ahead = [x + y for x, y in zip(here, beyond)]
                finish_cell(stage, c, [x + y for x, y in zip(joined, ahead)], 0.1)
                return beyond, ahead

            near, here = blurs(stage - 1, low - 1), blurs(stage - 1, low)
            lax.fori_loop(low, high, cell, (here, [x + y for x, y in zip(near, here)]), unroll=2)

        nothing = jnp.zeros(data_ref.shape[2:], jnp.float32)

        @pl.when(phi == 0)
        def _():
            for c in range(HALO):
                data_ref[b, c] = nothing

        @pl.when(phi == n_phi - 1)
        def _():
            for c in range(all_tilts - HALO, all_tilts):
                data_ref[b, c] = nothing

        def wait_for(places, back_tilt, step):
            for place in places:
                if last:
                    arrival(b, place, back_tilt, 1, last_recvs.at[place, step]).wait_recv()
                else:
                    arrival(b, place, 0, HALO, recv_sems.at[b, place]).wait_recv()

        def wait_step(step):
            @pl.when(has_before)
            def _():
                wait_for((2, 3), HALO - 1 - step, step)

            @pl.when(has_after)
            def _():
                wait_for((0, 1), step, step)

        if not last:
            wait_step(0)

        def wave(step, carry):
            if last:
                wait_step(step)
            tilts = (HALO - 1 - step, HALO + own_tilts + step)
            steps = (1, -1)
            adds = (left_add, right_add)
            chain = [keep_blur(0, c, first_estimate(c, add)) for c, add in zip(tilts, adds)]
            for stage in range(1, stages + 1):
                for side in range(2):
                    c = tilts[side] + steps[side] * stage
                    here, beyond = blurs(stage - 1, c), blurs(stage - 1, c + steps[side])
                    mixed = [(x + y) + (y + z) for x, y, z in zip(chain[side], here, beyond)]
                    outside = c < HALO if side == 0 else c >= HALO + own_tilts
                    chain[side] = finish_cell(stage, c, mixed, jnp.where(outside, adds[side], 0.1))
            return carry

        lax.fori_loop(0, HALO, wave, 0)

    def some_block(b, carry):
        block(b, False)
        return carry

    lax.fori_loop(0, blocks - 1, some_block, 0)
    block(blocks - 1, True)

    def finish(b, carry):
        with_neighbours(lambda number: halo_copy(b, number).wait_send())
        return carry

    lax.fori_loop(0, blocks - 1, finish, 0)

    def finish_last(step, carry):
        with_neighbours(lambda number: last_copy(number, step).wait_send())
        return carry

    lax.fori_loop(0, HALO, finish_last, 0)

    def finish_pair(b, carry):
        pair_copy(b, mine).wait_send()
        return carry

    lax.fori_loop(0, blocks, finish_pair, 0)


def body(n_phi, frames, drift_rows, drift_cols, weight_index, blur_band):
    tilts, own_phis, rows, cols = frames.shape
    pixels = blur_band.shape[0]
    phis = 2 * own_phis
    planes = pixels // LANES
    blocks = planes // SUBS
    tile = (SUBS, LANES)
    all_tilts = tilts + 2 * HALO
    hbm = pl.BlockSpec(memory_space=pltpu.HBM)
    table = pltpu.SMEM((own_phis, tilts), jnp.int32)
    out = pl.pallas_call(
        functools.partial(kernel, n_phi),
        out_shape=pltpu.VMEM((tilts, planes, phis, LANES), jnp.float32),
        in_specs=[hbm] * 5,
        out_specs=pl.BlockSpec(memory_space=pltpu.VMEM),
        scratch_shapes=[
            table,
            table,
            table,
            pltpu.VMEM((planes, LANES), jnp.int32),
            pltpu.VMEM(frames.shape, frames.dtype),
            pltpu.VMEM((own_phis, rows + 2 * PAD_ROWS, cols // LANES // SUBS) + tile, jnp.float32),
            pltpu.VMEM((2, blocks, tilts, own_phis) + tile, jnp.float32),
            pltpu.VMEM((blocks, all_tilts, phis) + tile, jnp.float32),
            pltpu.VMEM((all_tilts, phis) + tile, jnp.float32),
            pltpu.VMEM((2 * ITERS, all_tilts, phis) + tile, jnp.float32),
            pltpu.SemaphoreType.DMA((3,)),
            pltpu.SemaphoreType.DMA,
            pltpu.SemaphoreType.DMA((HALO, 2)),
            pltpu.SemaphoreType.DMA,
            pltpu.SemaphoreType.DMA((blocks - 1, REMOTE)),
            pltpu.SemaphoreType.DMA((blocks - 1, REMOTE)),
            pltpu.SemaphoreType.DMA((REMOTE, HALO)),
            pltpu.SemaphoreType.DMA((REMOTE, HALO)),
            pltpu.SemaphoreType.DMA((blocks,)),
            pltpu.SemaphoreType.DMA((blocks,)),
            pltpu.SemaphoreType.DMA((blocks,)),
        ],
        compiler_params=pltpu.CompilerParams(
            collective_id=0, has_side_effects=True, vmem_limit_bytes=56 * 1024 * 1024
        ),
        name="rocking",
    )(drift_rows.T, drift_cols.T, weight_index.T, blur_band.reshape(planes, LANES), frames)
    return out.transpose(0, 2, 1, 3).reshape(tilts, phis, pixels)


def solution(mesh):
    return jax.shard_map(
        functools.partial(body, mesh.shape["phi"]),
        mesh=mesh,
        in_specs=(
            P("phi", "chi", None, None),
            P("phi", "chi"),
            P("phi", "chi"),
            P("phi", "chi"),
            P("chi"),
        ),
        out_specs=P("phi", None, "chi"),
        check_vma=False,
    )
```

```python
import functools

import jax
import jax.numpy as jnp
from jax import lax
from jax.experimental import pallas as pl
from jax.experimental.pallas import tpu as pltpu
from jax.sharding import PartitionSpec as P

ITERS = 3
HALO = 2 * ITERS
LANES = 128
SUBS = 8
MOST_ROWS = 2
PAD_ROWS = MOST_ROWS + 1
ROW = 4
PLANE = 16
FORWARD_AT = 2
RELAYS = 2
REMOTE = 4


def shift_tilt(tilt, rows_ref, cols_ref, index_ref, frames_ref, spread_ref, staged_ref):
    own_phis, rows, cols = frames_ref.shape[1:]
    tiles = cols // LANES
    halves = tiles // SUBS
    blocks = staged_ref.shape[1]
    lane = lax.broadcasted_iota(jnp.int32, (rows, LANES), 1)
    zero = jnp.zeros((rows, LANES), jnp.float32)
    for p in range(own_phis):
        drift_col = cols_ref[p, tilt]
        frac_x = (index_ref[p, tilt] & 7).astype(jnp.float32) / 8.0
        turn = (drift_col + LANES) & (LANES - 1)
        from_left = lane < drift_col
        from_right = lane >= LANES + drift_col
        frame = frames_ref[tilt, p].astype(jnp.float32)
        source = [frame[:, t * LANES : (t + 1) * LANES] for t in range(tiles)] + [zero]
        stepped = [pltpu.roll(s, 1, 1) for s in source[:-1]]
        turned = []
        for t in range(tiles + 1):
            before = stepped[t - 1] if t > 0 else zero
            here = stepped[t] if t < tiles else zero
            mixed = (1.0 - frac_x) * source[t] + frac_x * jnp.where(lane < 1, before, here)
            turned.append(pltpu.roll(mixed, turn, 1))
        moved = []
        for t in range(tiles):
            left = turned[t - 1] if t > 0 else zero
            moved.append(jnp.where(from_left, left, jnp.where(from_right, turned[t + 1], turned[t])))
        for h in range(halves):
            group = jnp.stack(moved[h * SUBS : (h + 1) * SUBS])
            spread_ref[p, PAD_ROWS : PAD_ROWS + rows, h] = jnp.swapaxes(group, 0, 1)
    for p in range(own_phis):
        drift_row = jnp.clip(rows_ref[p, tilt], -MOST_ROWS, MOST_ROWS)
        frac_y = (index_ref[p, tilt] >> 3).astype(jnp.float32) / 8.0
        for r in range(rows):
            row = (1.0 - frac_y) * spread_ref[p, r + PAD_ROWS - drift_row] + frac_y * spread_ref[
                p, r + PAD_ROWS - 1 - drift_row
            ]
            for h in range(halves):
                place = r * halves + h
                staged_ref[place // blocks, place % blocks, tilt, p] = row[h]


def tap_matrices(band):
    spread = 0.8 + 0.6 * band.astype(jnp.float32)
    unnormed = [jnp.exp(-float(k * k) / (2.0 * spread * spread)) for k in range(5)]
    total = unnormed[0] + 2.0 * (unnormed[1] + unnormed[2] + unnormed[3] + unnormed[4])
    taps = [0.125 * (u / total) for u in unnormed]
    made = {}

    def pair(near, far, sign):
        if far > 4:
            return taps[near]
        if (near, far, sign) not in made:
            made[near, far, sign] = taps[near] + sign * taps[far] if near < far else taps[near] * 1.0 + sign * taps[far]
        return made[near, far, sign]

    even = [[pair(abs(p - q), 7 - p - q, 1.0) for q in range(4)] for p in range(4)]
    odd = [[pair(abs(p - q), 7 - p - q, -1.0) for q in range(4)] for p in range(4)]
    return even, odd


def phi_blur(tilts, even, odd):
    plus = [tilts[p] + tilts[7 - p] for p in range(4)]
    minus = [tilts[p] - tilts[7 - p] for p in range(4)]
    halves = []
    for matrix, parts in ((even, plus), (odd, minus)):
        rows = []
        for p in range(4):
            row = matrix[p][0] * parts[0]
            for q in range(1, 4):
                row = row + matrix[p][q] * parts[q]
            rows.append(row)
        halves.append(rows)
    front = [halves[0][p] + halves[1][p] for p in range(4)]
    back = [halves[0][3 - p] - halves[1][3 - p] for p in range(4)]
    return front + back


def kernel(
    n_phi,
    rows_hbm,
    cols_hbm,
    index_hbm,
    band_hbm,
    frames_hbm,
    out_ref,
    rows_ref,
    cols_ref,
    index_ref,
    band_ref,
    frames_ref,
    spread_ref,
    staged_ref,
    data_ref,
    estimate_ref,
    blurs_ref,
    table_sems,
    band_sem,
    edge_sems,
    middle_sem,
    send_sems,
    recv_sems,
    last_sends,
    last_recvs,
    relay_ref,
    relay_sends,
    relay_recvs,
    forward_sends,
    pair_sends,
    pair_recvs,
    local_sems,
):
    chi, phi = lax.axis_index("chi"), lax.axis_index("phi")
    other = 1 - chi
    before = lax.rem(phi + n_phi - 1, n_phi)
    after = lax.rem(phi + 1, n_phi)
    has_before, has_after = phi > 0, phi < n_phi - 1
    spot, plane = lax.rem(phi, PLANE), phi // PLANE
    planes = n_phi // PLANE
    own_tilts, own_phis = frames_ref.shape[:2]
    blocks, all_tilts, phis = data_ref.shape[:3]
    firsts = (0, own_tilts - HALO)

    def edge_load(tilt, side):
        at = firsts[side] + tilt
        return pltpu.make_async_copy(frames_hbm.at[at], frames_ref.at[at], edge_sems.at[tilt, side])

    tables = ((rows_hbm, rows_ref), (cols_hbm, cols_ref), (index_hbm, index_ref))
    table_loads = [pltpu.make_async_copy(a, b, table_sems.at[i]) for i, (a, b) in enumerate(tables)]
    for load in table_loads:
        load.start()
    for tilt in range(HALO):
        for side in (1, 0):
            edge_load(tilt, side).start()
    inner = pl.ds(HALO, own_tilts - 2 * HALO)
    middle_load = pltpu.make_async_copy(frames_hbm.at[inner], frames_ref.at[inner], middle_sem)
    middle_load.start()
    band_load = pltpu.make_async_copy(band_hbm, band_ref, band_sem)
    band_load.start()

    barrier = pltpu.get_barrier_semaphore()
    peers = [(before, 0), (before, 1), (after, 0), (after, 1)]

    def greet(to_phi, to_chi):
        pl.semaphore_signal(
            barrier, inc=1, device_id={"chi": to_chi, "phi": to_phi}, device_id_type=pl.DeviceIdType.MESH
        )

    def with_neighbours(act):
        @pl.when(has_before)
        def _():
            for number in (0, 1):
                act(number)

        @pl.when(has_after)
        def _():
            for number in (2, 3):
                act(number)

    def as_feeder(act):
        @pl.when(spot == PLANE - 1)
        def _():
            pl.when(plane < planes - 1)(act)

    def as_relay(k, act):
        @pl.when(spot == ROW * k + ROW - 1)
        def _():
            pl.when(plane > 0)(act)

    def as_fed(act):
        @pl.when(spot == 0)
        def _():
            pl.when(plane > 0)(act)

    def wrapped(to_phi):
        return lax.rem(to_phi + n_phi, n_phi)

    def greet_feeder(k):
        for to_chi in range(2):
            greet(wrapped(phi - ROW * (k + 1)), to_chi)

    def greet_relays():
        for k in range(RELAYS):
            greet(wrapped(phi + ROW * (k + 1) - 1), chi)

    with_neighbours(lambda number: greet(*peers[number]))
    greet(phi, other)
    for k in range(RELAYS):
        as_relay(k, functools.partial(greet_feeder, k))
    as_fed(greet_relays)
    one_plane_up = (plane > 0).astype(jnp.int32)
    feeding = (spot == PLANE - 1).astype(jnp.int32) * (plane < planes - 1).astype(jnp.int32)
    relaying = sum((spot == ROW * (k + 1) - 1).astype(jnp.int32) for k in range(RELAYS)) * one_plane_up
    greetings = 1 + 2 * has_before.astype(jnp.int32) + 2 * has_after.astype(jnp.int32)
    greetings = greetings + 2 * RELAYS * feeding + relaying

    empty = jnp.zeros(spread_ref.shape[2:], jnp.float32)
    for p in range(own_phis):
        for r in range(PAD_ROWS):
            spread_ref[p, r] = empty
            spread_ref[p, spread_ref.shape[1] - 1 - r] = empty

    mine = pl.ds(chi * own_phis, own_phis)

    def neighbour_copy(b, number, tilt, tilts, send_sem, recv_sem, flip):
        back = number < 2
        to_chi = lax.rem(flip + number, 2)
        first = 0 if back else own_tilts - HALO
        first_there = all_tilts - HALO if back else 0
        return pltpu.make_async_remote_copy(
            src_ref=staged_ref.at[to_chi, b, pl.ds(first + tilt, tilts)],
            dst_ref=data_ref.at[b, pl.ds(first_there + tilt, tilts), mine],
            send_sem=send_sem,
            recv_sem=recv_sem,
            device_id={"chi": to_chi, "phi": before if back else after},
            device_id_type=pl.DeviceIdType.MESH,
        )

    def place_of(number):
        return (0 if number < 2 else 2) + chi

    def halo_copy(b, number, tilt=0, tilts=HALO):
        return neighbour_copy(b, number, tilt, tilts, send_sems.at[b, number], recv_sems.at[b, place_of(number)], b)

    def last_copy(number, step):
        tilt = step if number < 2 else HALO - 1 - step
        return neighbour_copy(
            blocks - 1, number, tilt, 1, last_sends.at[number, step], last_recvs.at[place_of(number), step], step
        )

    def arrival(b, place, tilt, tilts, recv_sem):
        back = place < 2
        from_chi = place % 2
        first = all_tilts - HALO if back else 0
        return pltpu.make_async_remote_copy(
            src_ref=staged_ref.at[0, b, pl.ds(0, tilts)],
            dst_ref=data_ref.at[b, pl.ds(first + tilt, tilts), pl.ds(from_chi * own_phis, own_phis)],
            send_sem=send_sems.at[0, place],
            recv_sem=recv_sem,
            device_id={"chi": from_chi, "phi": after if back else before},
            device_id_type=pl.DeviceIdType.MESH,
        )

    middle = pl.ds(HALO, own_tilts)

    def pair_copy(b, phis_at):
        return pltpu.make_async_remote_copy(
            src_ref=staged_ref.at[other, b],
            dst_ref=data_ref.at[b, middle, phis_at],
            send_sem=pair_sends.at[b],
            recv_sem=pair_recvs.at[b],
            device_id={"chi": other, "phi": phi},
            device_id_type=pl.DeviceIdType.MESH,
        )

    def local_copy(b):
        return pltpu.make_async_copy(staged_ref.at[chi, b], data_ref.at[b, middle, mine], local_sems.at[b])

    def shift_at(tilt):
        shift_tilt(tilt, rows_ref, cols_ref, index_ref, frames_ref, spread_ref, staged_ref)

    for load in table_loads:
        load.wait()

    def shift_edges(tilt, carry):
        for side in (1, 0):
            edge_load(tilt, side).wait()
            shift_at(firsts[side] + tilt)

        @pl.when(tilt == 0)
        def _():
            pl.semaphore_wait(barrier, greetings)

        with_neighbours(lambda number: halo_copy(0, number, tilt, 1).start())
        return carry

    lax.fori_loop(0, HALO, shift_edges, 0)

    def send_halos(b, carry):
        with_neighbours(lambda number: halo_copy(b, number).start())
        return carry

    lax.fori_loop(1, blocks - 1, send_halos, 0)

    def relay_copy(k, to_chi):
        return pltpu.make_async_remote_copy(
            src_ref=staged_ref.at[to_chi, blocks - 1, pl.ds(own_tilts - HALO + k, 1)],
            dst_ref=relay_ref.at[chi],
            send_sem=relay_sends.at[k, to_chi],
            recv_sem=relay_recvs.at[chi],
            device_id={"chi": to_chi, "phi": wrapped(phi + ROW * (k + 1))},
            device_id_type=pl.DeviceIdType.MESH,
        )

    def forward_copy(k, from_chi):
        return pltpu.make_async_remote_copy(
            src_ref=relay_ref.at[from_chi],
            dst_ref=data_ref.at[blocks - 1, pl.ds(k, 1), pl.ds(from_chi * own_phis, own_phis)],
            send_sem=forward_sends.at[from_chi],
            recv_sem=last_recvs.at[2 + from_chi, HALO - 1 - k],
            device_id={"chi": chi, "phi": wrapped(phi - ROW * (k + 1) + 1)},
            device_id_type=pl.DeviceIdType.MESH,
        )

    def relay_arrival(from_chi):
        return pltpu.make_async_remote_copy(
            src_ref=staged_ref.at[0, 0, pl.ds(0, 1)],
            dst_ref=relay_ref.at[from_chi],
            send_sem=relay_sends.at[0, from_chi],
            recv_sem=relay_recvs.at[from_chi],
            device_id={"chi": from_chi, "phi": wrapped(phi - ROW)},
            device_id_type=pl.DeviceIdType.MESH,
        )

    def each_relay_copy(act):
        for k in range(RELAYS):
            for to_chi in range(2):
                act(relay_copy(k, to_chi))

    def forward(k):
        for from_chi in range(2):
            relay_arrival(from_chi).wait_recv()
            forward_copy(k, from_chi).start()

    as_feeder(lambda: each_relay_copy(lambda copy: copy.start()))
    direct = HALO - RELAYS * feeding

    def with_last(step, act):
        @pl.when(has_before)
        def _():
            for number in (0, 1):
                act(number)

        @pl.when(has_after)
        def _():
            @pl.when(step < direct)
            def _():
                for number in (2, 3):
                    act(number)

    def send_last(step, carry):
        with_last(step, lambda number: last_copy(number, step).start())
        return carry

    lax.fori_loop(0, HALO, send_last, 0)
    middle_load.wait()

    def shift_inner(tilt, carry):
        shift_at(tilt)
        return carry

    lax.fori_loop(HALO, own_tilts - HALO, shift_inner, 0)

    def send_pairs(b, carry):
        pair_copy(b, mine).start()
        local_copy(b).start()
        return carry

    lax.fori_loop(0, blocks, send_pairs, 0)
    band_load.wait()

    left_add = jnp.where(phi == 0, 0.0, 0.1)
    right_add = jnp.where(phi == n_phi - 1, 0.0, 0.1)

    def block(b, last):
        even, odd = tap_matrices(band_ref[pl.ds(pl.multiple_of(b * SUBS, SUBS), SUBS), :])
        stages = 2 * ITERS

        def blurs(stage, c):
            return [blurs_ref[stage, c, p] for p in range(phis)]

        def keep_blur(stage, c, values):
            made = phi_blur(values, even, odd)
            for p in range(phis):
                blurs_ref[stage, c, p] = made[p]
            return made

        def first_estimate(c, add):
            return [data_ref[b, c, p] + add for p in range(phis)]

        def finish_cell(stage, c, mixed, add):
            if stage % 2 == 1:
                made = [data_ref[b, c, p] / (mixed[p] + 0.1) for p in range(phis)]
            else:
                old = first_estimate(c, add) if stage == 2 else [estimate_ref[c, p] for p in range(phis)]
                made = [o * m for o, m in zip(old, mixed)]
                if stage < stages:
                    for p in range(phis):
                        estimate_ref[c, p] = made[p]
            if stage < stages:
                return keep_blur(stage, c, made)
            rows_at = pl.ds(pl.multiple_of(b * SUBS, SUBS), SUBS)
            out_ref[c - HALO, rows_at] = jnp.swapaxes(jnp.stack(made), 0, 1)
            return made

        pair_copy(b, pl.ds(other * own_phis, own_phis)).wait_recv()
        local_copy(b).wait()

        def start_cell(c, carry):
            keep_blur(0, c, first_estimate(c, 0.1))
            return carry

        lax.fori_loop(HALO, HALO + own_tilts, start_cell, 0, unroll=2)
        for stage in range(1, stages + 1):
            low, high = HALO + stage, HALO + own_tilts - stage

            def cell(c, carry):
                here, joined = carry
                beyond = blurs(stage - 1, c + 1)
                ahead = [x + y for x, y in zip(here, beyond)]
                finish_cell(stage, c, [x + y for x, y in zip(joined, ahead)], 0.1)
                return beyond, ahead

            near, here = blurs(stage - 1, low - 1), blurs(stage - 1, low)
            lax.fori_loop(low, high, cell, (here, [x + y for x, y in zip(near, here)]), unroll=2)

        nothing = jnp.zeros(data_ref.shape[2:], jnp.float32)

        @pl.when(phi == 0)
        def _():
            for c in range(HALO):
                data_ref[b, c] = nothing

        @pl.when(phi == n_phi - 1)
        def _():
            for c in range(all_tilts - HALO, all_tilts):
                data_ref[b, c] = nothing

        def wait_for(places, back_tilt, step):
            for place in places:
                if last:
                    arrival(b, place, back_tilt, 1, last_recvs.at[place, step]).wait_recv()
                else:
                    arrival(b, place, 0, HALO, recv_sems.at[b, place]).wait_recv()

        def wait_step(step):
            @pl.when(has_before)
            def _():
                wait_for((2, 3), HALO - 1 - step, step)

            @pl.when(has_after)
            def _():
                wait_for((0, 1), step, step)

        if not last:
            wait_step(0)

        def wave(step, carry):
            if last:
                wait_step(step)
            tilts = (HALO - 1 - step, HALO + own_tilts + step)
            steps = (1, -1)
            adds = (left_add, right_add)
            chain = [keep_blur(0, c, first_estimate(c, add)) for c, add in zip(tilts, adds)]
            for stage in range(1, stages + 1):
                for side in range(2):
                    c = tilts[side] + steps[side] * stage
                    here, beyond = blurs(stage - 1, c), blurs(stage - 1, c + steps[side])
                    mixed = [(x + y) + (y + z) for x, y, z in zip(chain[side], here, beyond)]
                    outside = c < HALO if side == 0 else c >= HALO + own_tilts
                    chain[side] = finish_cell(stage, c, mixed, jnp.where(outside, adds[side], 0.1))
            return carry

        lax.fori_loop(0, HALO, wave, 0)

    def some_block(b, carry):
        @pl.when(b == FORWARD_AT)
        def _():
            for k in range(RELAYS):
                as_relay(k, functools.partial(forward, k))

        block(b, False)
        return carry

    lax.fori_loop(0, blocks - 1, some_block, 0)
    block(blocks - 1, True)

    def finish(b, carry):
        with_neighbours(lambda number: halo_copy(b, number).wait_send())
        return carry

    lax.fori_loop(0, blocks - 1, finish, 0)

    def finish_last(step, carry):
        with_last(step, lambda number: last_copy(number, step).wait_send())
        return carry

    lax.fori_loop(0, HALO, finish_last, 0)
    as_feeder(lambda: each_relay_copy(lambda copy: copy.wait_send()))

    def finish_forward(k):
        for from_chi in range(2):
            forward_copy(k, from_chi).wait_send()

    for k in range(RELAYS):
        as_relay(k, functools.partial(finish_forward, k))

    def finish_pair(b, carry):
        pair_copy(b, mine).wait_send()
        return carry

    lax.fori_loop(0, blocks, finish_pair, 0)


def body(n_phi, frames, drift_rows, drift_cols, weight_index, blur_band):
    tilts, own_phis, rows, cols = frames.shape
    pixels = blur_band.shape[0]
    phis = 2 * own_phis
    planes = pixels // LANES
    blocks = planes // SUBS
    tile = (SUBS, LANES)
    all_tilts = tilts + 2 * HALO
    hbm = pl.BlockSpec(memory_space=pltpu.HBM)
    table = pltpu.SMEM((own_phis, tilts), jnp.int32)
    out = pl.pallas_call(
        functools.partial(kernel, n_phi),
        out_shape=pltpu.VMEM((tilts, planes, phis, LANES), jnp.float32),
        in_specs=[hbm] * 5,
        out_specs=pl.BlockSpec(memory_space=pltpu.VMEM),
        scratch_shapes=[
            table,
            table,
            table,
            pltpu.VMEM((planes, LANES), jnp.int32),
            pltpu.VMEM(frames.shape, frames.dtype),
            pltpu.VMEM((own_phis, rows + 2 * PAD_ROWS, cols // LANES // SUBS) + tile, jnp.float32),
            pltpu.VMEM((2, blocks, tilts, own_phis) + tile, jnp.float32),
            pltpu.VMEM((blocks, all_tilts, phis) + tile, jnp.float32),
            pltpu.VMEM((all_tilts, phis) + tile, jnp.float32),
            pltpu.VMEM((2 * ITERS, all_tilts, phis) + tile, jnp.float32),
            pltpu.SemaphoreType.DMA((3,)),
            pltpu.SemaphoreType.DMA,
            pltpu.SemaphoreType.DMA((HALO, 2)),
            pltpu.SemaphoreType.DMA,
            pltpu.SemaphoreType.DMA((blocks - 1, REMOTE)),
            pltpu.SemaphoreType.DMA((blocks - 1, REMOTE)),
            pltpu.SemaphoreType.DMA((REMOTE, HALO)),
            pltpu.SemaphoreType.DMA((REMOTE, HALO)),
            pltpu.VMEM((2, 1, own_phis) + tile, jnp.float32),
            pltpu.SemaphoreType.DMA((RELAYS, 2)),
            pltpu.SemaphoreType.DMA((2,)),
            pltpu.SemaphoreType.DMA((2,)),
            pltpu.SemaphoreType.DMA((blocks,)),
            pltpu.SemaphoreType.DMA((blocks,)),
            pltpu.SemaphoreType.DMA((blocks,)),
        ],
        compiler_params=pltpu.CompilerParams(
            collective_id=0, has_side_effects=True, vmem_limit_bytes=56 * 1024 * 1024
        ),
        name="rocking",
    )(drift_rows.T, drift_cols.T, weight_index.T, blur_band.reshape(planes, LANES), frames)
    return out.transpose(0, 2, 1, 3).reshape(tilts, phis, pixels)


def solution(mesh):
    return jax.shard_map(
        functools.partial(body, mesh.shape["phi"]),
        mesh=mesh,
        in_specs=(
            P("phi", "chi", None, None),
            P("phi", "chi"),
            P("phi", "chi"),
            P("phi", "chi"),
            P("chi"),
        ),
        out_specs=P("phi", None, "chi"),
        check_vma=False,
    )
```

```python
import functools

import jax
import jax.numpy as jnp
from jax import lax
from jax.experimental import pallas as pl
from jax.experimental.pallas import tpu as pltpu
from jax.sharding import PartitionSpec as P

ITERS = 3
STAGES = 2 * ITERS
HALO = STAGES
LANES = 128
SUBS = 8
MOST_ROWS = 2
PAD_ROWS = MOST_ROWS + 1
REMOTE = 4


def shift_tilt(tilt, rows_ref, cols_ref, index_ref, frames_ref, spread_ref, staged_ref):
    own_phis, rows, cols = frames_ref.shape[1:]
    tiles = cols // LANES
    halves = tiles // SUBS
    blocks = staged_ref.shape[1]
    lane = lax.broadcasted_iota(jnp.int32, (rows, LANES), 1)
    zero = jnp.zeros((rows, LANES), jnp.float32)
    for p in range(own_phis):
        drift_col = cols_ref[p, tilt]
        frac_x = (index_ref[p, tilt] & 7).astype(jnp.float32) / 8.0
        turn = (drift_col + LANES) & (LANES - 1)
        from_left = lane < drift_col
        from_right = lane >= LANES + drift_col
        frame = frames_ref[tilt, p].astype(jnp.float32)
        source = [frame[:, t * LANES : (t + 1) * LANES] for t in range(tiles)] + [zero]
        stepped = [pltpu.roll(s, 1, 1) for s in source[:-1]]
        turned = []
        for t in range(tiles + 1):
            before = stepped[t - 1] if t > 0 else zero
            here = stepped[t] if t < tiles else zero
            mixed = (1.0 - frac_x) * source[t] + frac_x * jnp.where(lane < 1, before, here)
            turned.append(pltpu.roll(mixed, turn, 1))
        moved = []
        for t in range(tiles):
            left = turned[t - 1] if t > 0 else zero
            moved.append(jnp.where(from_left, left, jnp.where(from_right, turned[t + 1], turned[t])))
        for h in range(halves):
            group = jnp.stack(moved[h * SUBS : (h + 1) * SUBS])
            spread_ref[p, PAD_ROWS : PAD_ROWS + rows, h] = jnp.swapaxes(group, 0, 1)
    for p in range(own_phis):
        drift_row = jnp.clip(rows_ref[p, tilt], -MOST_ROWS, MOST_ROWS)
        frac_y = (index_ref[p, tilt] >> 3).astype(jnp.float32) / 8.0
        for r in range(rows):
            row = (1.0 - frac_y) * spread_ref[p, r + PAD_ROWS - drift_row] + frac_y * spread_ref[
                p, r + PAD_ROWS - 1 - drift_row
            ]
            for h in range(halves):
                place = r * halves + h
                staged_ref[place // blocks, place % blocks, tilt, p] = row[h]


def tap_matrices(band):
    spread = 0.8 + 0.6 * band.astype(jnp.float32)
    unnormed = [jnp.exp(-float(k * k) / (2.0 * spread * spread)) for k in range(5)]
    total = unnormed[0] + 2.0 * (unnormed[1] + unnormed[2] + unnormed[3] + unnormed[4])
    taps = [0.125 * (u / total) for u in unnormed]
    made = {}

    def pair(near, far, sign):
        if far > 4:
            return taps[near]
        if (near, far, sign) not in made:
            made[near, far, sign] = taps[near] + sign * taps[far] if near < far else taps[near] * 1.0 + sign * taps[far]
        return made[near, far, sign]

    even = [[pair(abs(p - q), 7 - p - q, 1.0) for q in range(4)] for p in range(4)]
    odd = [[pair(abs(p - q), 7 - p - q, -1.0) for q in range(4)] for p in range(4)]
    return even, odd


def phi_blur(tilts, even, odd):
    plus = [tilts[p] + tilts[7 - p] for p in range(4)]
    minus = [tilts[p] - tilts[7 - p] for p in range(4)]
    halves = []
    for matrix, parts in ((even, plus), (odd, minus)):
        rows = []
        for p in range(4):
            row = matrix[p][0] * parts[0]
            for q in range(1, 4):
                row = row + matrix[p][q] * parts[q]
            rows.append(row)
        halves.append(rows)
    front = [halves[0][p] + halves[1][p] for p in range(4)]
    back = [halves[0][3 - p] - halves[1][3 - p] for p in range(4)]
    return front + back


def cells(data_ref, estimate_ref, blurs_ref, even, odd, emit):
    phis = data_ref.shape[1]

    def blurs(stage, c):
        return [blurs_ref[stage, c, p] for p in range(phis)]

    def keep_blur(stage, c, values, keep=True):
        made = phi_blur(values, even, odd)
        if keep:
            for p in range(phis):
                blurs_ref[stage, c, p] = made[p]
        return made

    def first_estimate(c, add):
        return [data_ref[c, p] + add for p in range(phis)]

    def finish_cell(stage, c, mixed, add, keep=True):
        if stage % 2 == 1:
            made = [data_ref[c, p] / (mixed[p] + 0.1) for p in range(phis)]
        else:
            old = first_estimate(c, add) if stage == 2 else [estimate_ref[c, p] for p in range(phis)]
            made = [o * m for o, m in zip(old, mixed)]
            if stage < STAGES and keep:
                for p in range(phis):
                    estimate_ref[c, p] = made[p]
        if stage < STAGES:
            return keep_blur(stage, c, made, keep)
        emit(c, jnp.swapaxes(jnp.stack(made), 0, 1))
        return made

    return blurs, keep_blur, first_estimate, finish_cell


def run_wave(step, own_tilts, adds, helpers, keep=True):
    blurs, keep_blur, first_estimate, finish_cell = helpers
    tilts = (HALO - 1 - step, HALO + own_tilts + step)
    steps = (1, -1)
    chain = [keep_blur(0, c, first_estimate(c, add), keep) for c, add in zip(tilts, adds)]
    for stage in range(1, STAGES + 1):
        for side in range(2):
            c = tilts[side] + steps[side] * stage
            here, beyond = blurs(stage - 1, c), blurs(stage - 1, c + steps[side])
            mixed = [(x + y) + (y + z) for x, y, z in zip(chain[side], here, beyond)]
            outside = c < HALO if side == 0 else c >= HALO + own_tilts
            chain[side] = finish_cell(stage, c, mixed, jnp.where(outside, adds[side], 0.1), keep)


def end_adds(n_phi):
    phi = lax.axis_index("phi")
    return jnp.where(phi == 0, 0.0, 0.1), jnp.where(phi == n_phi - 1, 0.0, 0.1)


def deliver(n_phi, source_ref, data_ref, estimate_ref, blurs_ref, band_ref, out_hbm, edge_ref, sems, edge_sems):
    tilts, planes = source_ref.shape[:2]
    blocks = planes // SUBS
    copies = []
    for t in range(tilts):
        part = pl.ds(0, planes - SUBS if t in (0, tilts - 1) else planes)
        copies.append(pltpu.make_async_copy(source_ref.at[t, part], out_hbm.at[t, part], sems.at[t]))
        copies[-1].start()

    def emit(c, made):
        edge_ref[0 if c == HALO else 1] = made

    even, odd = tap_matrices(band_ref[...])
    helpers = cells(data_ref.at[blocks - 1], estimate_ref, blurs_ref, even, odd, emit)
    run_wave(HALO - 1, tilts, end_adds(n_phi), helpers, keep=False)
    for side, t in enumerate((0, tilts - 1)):
        part = pl.ds(planes - SUBS, SUBS)
        copies.append(pltpu.make_async_copy(edge_ref.at[side], out_hbm.at[t, part], edge_sems.at[side]))
        copies[-1].start()
    for copy in copies:
        copy.wait()


def kernel(
    n_phi,
    rows_hbm,
    cols_hbm,
    index_hbm,
    band_hbm,
    frames_hbm,
    out_ref,
    data_ref,
    estimate_ref,
    blurs_ref,
    last_band_ref,
    rows_ref,
    cols_ref,
    index_ref,
    band_ref,
    frames_ref,
    spread_ref,
    staged_ref,
    table_sems,
    band_sem,
    edge_sems,
    middle_sem,
    send_sems,
    recv_sems,
    last_sends,
    last_recvs,
    pair_sends,
    pair_recvs,
    local_sems,
):
    chi, phi = lax.axis_index("chi"), lax.axis_index("phi")
    other = 1 - chi
    before = lax.rem(phi + n_phi - 1, n_phi)
    after = lax.rem(phi + 1, n_phi)
    has_before, has_after = phi > 0, phi < n_phi - 1
    own_tilts, own_phis = frames_ref.shape[:2]
    blocks, all_tilts, phis = data_ref.shape[:3]
    firsts = (0, own_tilts - HALO)

    def edge_load(tilt, side):
        at = firsts[side] + tilt
        return pltpu.make_async_copy(frames_hbm.at[at], frames_ref.at[at], edge_sems.at[tilt, side])

    barrier = pltpu.get_barrier_semaphore()
    peers = [(before, 0), (before, 1), (after, 0), (after, 1)]

    def greet(to_phi, to_chi):
        pl.semaphore_signal(
            barrier, inc=1, device_id={"chi": to_chi, "phi": to_phi}, device_id_type=pl.DeviceIdType.MESH
        )

    def with_neighbours(act):
        for numbers in ((0, 2), (1, 3)):
            @pl.when(has_before)
            def _():
                act(numbers[0])

            @pl.when(has_after)
            def _():
                act(numbers[1])

    with_neighbours(lambda number: greet(*peers[number]))
    greet(phi, other)

    tables = ((rows_hbm, rows_ref), (cols_hbm, cols_ref), (index_hbm, index_ref))
    table_loads = [pltpu.make_async_copy(a, b, table_sems.at[i]) for i, (a, b) in enumerate(tables)]
    for load in table_loads:
        load.start()
    for tilt in range(HALO):
        for side in (1, 0):
            edge_load(tilt, side).start()
    inner = pl.ds(HALO, own_tilts - 2 * HALO)
    middle_load = pltpu.make_async_copy(frames_hbm.at[inner], frames_ref.at[inner], middle_sem)
    middle_load.start()
    band_load = pltpu.make_async_copy(band_hbm, band_ref, band_sem)
    band_load.start()

    empty = jnp.zeros(spread_ref.shape[2:], jnp.float32)
    for p in range(own_phis):
        for r in range(PAD_ROWS):
            spread_ref[p, r] = empty
            spread_ref[p, spread_ref.shape[1] - 1 - r] = empty

    mine = pl.ds(chi * own_phis, own_phis)

    def neighbour_copy(b, number, tilt, tilts, send_sem, recv_sem, flip):
        back = number < 2
        to_chi = lax.rem(flip + number, 2)
        first = 0 if back else own_tilts - HALO
        first_there = all_tilts - HALO if back else 0
        return pltpu.make_async_remote_copy(
            src_ref=staged_ref.at[to_chi, b, pl.ds(first + tilt, tilts)],
            dst_ref=data_ref.at[b, pl.ds(first_there + tilt, tilts), mine],
            send_sem=send_sem,
            recv_sem=recv_sem,
            device_id={"chi": to_chi, "phi": before if back else after},
            device_id_type=pl.DeviceIdType.MESH,
        )

    def place_of(number):
        return (0 if number < 2 else 2) + chi

    def halo_copy(b, number, tilt=0, tilts=HALO):
        return neighbour_copy(b, number, tilt, tilts, send_sems.at[b, number], recv_sems.at[b, place_of(number)], b)

    def last_copy(number, step):
        tilt = step if number < 2 else HALO - 1 - step
        return neighbour_copy(
            blocks - 1, number, tilt, 1, last_sends.at[number, step], last_recvs.at[place_of(number), step], step
        )

    def arrival(b, place, tilt, tilts, recv_sem):
        back = place < 2
        from_chi = place % 2
        first = all_tilts - HALO if back else 0
        return pltpu.make_async_remote_copy(
            src_ref=staged_ref.at[0, b, pl.ds(0, tilts)],
            dst_ref=data_ref.at[b, pl.ds(first + tilt, tilts), pl.ds(from_chi * own_phis, own_phis)],
            send_sem=send_sems.at[0, place],
            recv_sem=recv_sem,
            device_id={"chi": from_chi, "phi": after if back else before},
            device_id_type=pl.DeviceIdType.MESH,
        )

    middle = pl.ds(HALO, own_tilts)

    def pair_copy(b, phis_at):
        return pltpu.make_async_remote_copy(
            src_ref=staged_ref.at[other, b],
            dst_ref=data_ref.at[b, middle, phis_at],
            send_sem=pair_sends.at[b],
            recv_sem=pair_recvs.at[b],
            device_id={"chi": other, "phi": phi},
            device_id_type=pl.DeviceIdType.MESH,
        )

    def local_copy(b):
        return pltpu.make_async_copy(staged_ref.at[chi, b], data_ref.at[b, middle, mine], local_sems.at[b])

    def shift_at(tilt):
        shift_tilt(tilt, rows_ref, cols_ref, index_ref, frames_ref, spread_ref, staged_ref)

    for load in table_loads:
        load.wait()

    def shift_edges(tilt, carry):
        for side in (1, 0):
            edge_load(tilt, side).wait()
            shift_at(firsts[side] + tilt)

        @pl.when(tilt == 0)
        def _():
            pl.semaphore_wait(barrier, 1 + 2 * has_before.astype(jnp.int32) + 2 * has_after.astype(jnp.int32))

        with_neighbours(lambda number: halo_copy(0, number, tilt, 1).start())
        return carry

    lax.fori_loop(0, HALO, shift_edges, 0)

    def send_halos(b, carry):
        with_neighbours(lambda number: halo_copy(b, number).start())
        return carry

    lax.fori_loop(1, blocks - 1, send_halos, 0)

    def send_last(step, carry):
        with_neighbours(lambda number: last_copy(number, step).start())
        return carry

    lax.fori_loop(0, HALO, send_last, 0)
    middle_load.wait()

    def shift_inner(tilt, carry):
        shift_at(tilt)
        return carry

    lax.fori_loop(HALO, own_tilts - HALO, shift_inner, 0)

    def send_pairs(b, carry):
        pair_copy(b, mine).start()
        local_copy(b).start()
        return carry

    lax.fori_loop(0, blocks, send_pairs, 0)
    band_load.wait()

    adds = end_adds(n_phi)

    def block(b, last):
        even, odd = tap_matrices(band_ref[pl.ds(pl.multiple_of(b * SUBS, SUBS), SUBS), :])
        rows_at = pl.ds(pl.multiple_of(b * SUBS, SUBS), SUBS)

        def emit(c, made):
            out_ref[c - HALO, rows_at] = made

        blurs, keep_blur, first_estimate, finish_cell = cells(
            data_ref.at[b], estimate_ref, blurs_ref, even, odd, emit
        )

        pair_copy(b, pl.ds(other * own_phis, own_phis)).wait_recv()
        local_copy(b).wait()

        def start_cell(c, carry):
            keep_blur(0, c, first_estimate(c, 0.1))
            return carry

        lax.fori_loop(HALO, HALO + own_tilts, start_cell, 0, unroll=2)
        for stage in range(1, STAGES + 1):
            low, high = HALO + stage, HALO + own_tilts - stage

            def cell(c, carry):
                here, joined = carry
                beyond = blurs(stage - 1, c + 1)
                ahead = [x + y for x, y in zip(here, beyond)]
                finish_cell(stage, c, [x + y for x, y in zip(joined, ahead)], 0.1)
                return beyond, ahead

            near, here = blurs(stage - 1, low - 1), blurs(stage - 1, low)
            lax.fori_loop(low, high, cell, (here, [x + y for x, y in zip(near, here)]), unroll=2)

        nothing = jnp.zeros(data_ref.shape[2:], jnp.float32)

        @pl.when(phi == 0)
        def _():
            for c in range(HALO):
                data_ref[b, c] = nothing

        @pl.when(phi == n_phi - 1)
        def _():
            for c in range(all_tilts - HALO, all_tilts):
                data_ref[b, c] = nothing

        def wait_for(places, back_tilt, step):
            for place in places:
                if last:
                    arrival(b, place, back_tilt, 1, last_recvs.at[place, step]).wait_recv()
                else:
                    arrival(b, place, 0, HALO, recv_sems.at[b, place]).wait_recv()

        def wait_step(step):
            @pl.when(has_before)
            def _():
                wait_for((2, 3), HALO - 1 - step, step)

            @pl.when(has_after)
            def _():
                wait_for((0, 1), step, step)

        if not last:
            wait_step(0)

        helpers = blurs, keep_blur, first_estimate, finish_cell

        def wave(step, carry):
            if last:
                wait_step(step)
            run_wave(step, own_tilts, adds, helpers)
            return carry

        lax.fori_loop(0, HALO - 1 if last else HALO, wave, 0)
        if last:
            last_band_ref[...] = band_ref[rows_at, :]
            wait_step(HALO - 1)

    def some_block(b, carry):
        block(b, False)
        return carry

    lax.fori_loop(0, blocks - 1, some_block, 0)
    block(blocks - 1, True)

    def finish(b, carry):
        with_neighbours(lambda number: halo_copy(b, number).wait_send())
        return carry

    lax.fori_loop(0, blocks - 1, finish, 0)

    def finish_last(step, carry):
        with_neighbours(lambda number: last_copy(number, step).wait_send())
        return carry

    lax.fori_loop(0, HALO, finish_last, 0)

    def finish_pair(b, carry):
        pair_copy(b, mine).wait_send()
        return carry

    lax.fori_loop(0, blocks, finish_pair, 0)


def body(n_phi, frames, drift_rows, drift_cols, weight_index, blur_band):
    tilts, own_phis, rows, cols = frames.shape
    pixels = blur_band.shape[0]
    phis = 2 * own_phis
    planes = pixels // LANES
    blocks = planes // SUBS
    tile = (SUBS, LANES)
    all_tilts = tilts + 2 * HALO
    hbm = pl.BlockSpec(memory_space=pltpu.HBM)
    table = pltpu.SMEM((own_phis, tilts), jnp.int32)
    vmem = pl.BlockSpec(memory_space=pltpu.VMEM)
    held = pl.pallas_call(
        functools.partial(kernel, n_phi),
        out_shape=(
            pltpu.VMEM((tilts, planes, phis, LANES), jnp.float32),
            pltpu.VMEM((blocks, all_tilts, phis) + tile, jnp.float32),
            pltpu.VMEM((all_tilts, phis) + tile, jnp.float32),
            pltpu.VMEM((STAGES, all_tilts, phis) + tile, jnp.float32),
            pltpu.VMEM(tile, jnp.int32),
        ),
        in_specs=[hbm] * 5,
        out_specs=(vmem,) * 5,
        scratch_shapes=[
            table,
            table,
            table,
            pltpu.VMEM((planes, LANES), jnp.int32),
            pltpu.VMEM(frames.shape, frames.dtype),
            pltpu.VMEM((own_phis, rows + 2 * PAD_ROWS, cols // LANES // SUBS) + tile, jnp.float32),
            pltpu.VMEM((2, blocks, tilts, own_phis) + tile, jnp.float32),
            pltpu.SemaphoreType.DMA((3,)),
            pltpu.SemaphoreType.DMA,
            pltpu.SemaphoreType.DMA((HALO, 2)),
            pltpu.SemaphoreType.DMA,
            pltpu.SemaphoreType.DMA((blocks - 1, REMOTE)),
            pltpu.SemaphoreType.DMA((blocks - 1, REMOTE)),
            pltpu.SemaphoreType.DMA((REMOTE, HALO)),
            pltpu.SemaphoreType.DMA((REMOTE, HALO)),
            pltpu.SemaphoreType.DMA((blocks,)),
            pltpu.SemaphoreType.DMA((blocks,)),
            pltpu.SemaphoreType.DMA((blocks,)),
        ],
        compiler_params=pltpu.CompilerParams(
            collective_id=0, has_side_effects=True, vmem_limit_bytes=45 * 1024 * 1024
        ),
        name="rocking",
    )(drift_rows.T, drift_cols.T, weight_index.T, blur_band.reshape(planes, LANES), frames)
    held = [pltpu.with_memory_space_constraint(part, pltpu.VMEM) for part in held]
    out = pl.pallas_call(
        functools.partial(deliver, n_phi),
        out_shape=jax.ShapeDtypeStruct((tilts, planes, phis, LANES), jnp.float32),
        in_specs=[vmem] * 5,
        out_specs=hbm,
        scratch_shapes=[
            pltpu.VMEM((2, SUBS, phis, LANES), jnp.float32),
            pltpu.SemaphoreType.DMA((tilts,)),
            pltpu.SemaphoreType.DMA((2,)),
        ],
        compiler_params=pltpu.CompilerParams(vmem_limit_bytes=16 * 1024 * 1024),
        name="deliver",
    )(*held)
    return out.transpose(0, 2, 1, 3).reshape(tilts, phis, pixels)


def solution(mesh):
    return jax.shard_map(
        functools.partial(body, mesh.shape["phi"]),
        mesh=mesh,
        in_specs=(
            P("phi", "chi", None, None),
            P("phi", "chi"),
            P("phi", "chi"),
            P("phi", "chi"),
            P("chi"),
        ),
        out_specs=P("phi", None, "chi"),
        check_vma=False,
    )
```

```python
import functools

import jax
import jax.numpy as jnp
from jax import lax
from jax.experimental import pallas as pl
from jax.experimental.pallas import tpu as pltpu
from jax.sharding import PartitionSpec as P

ITERS = 3
STAGES = 2 * ITERS
HALO = STAGES
LANES = 128
SUBS = 8
MOST_ROWS = 2
PAD_ROWS = MOST_ROWS + 1
PLANE = 16
EARLY = 3
REMOTE = 4


def shift_tilt(tilt, rows_ref, cols_ref, index_ref, frames_ref, spread_ref, staged_ref):
    own_phis, rows, cols = frames_ref.shape[1:]
    tiles = cols // LANES
    halves = tiles // SUBS
    blocks = staged_ref.shape[1]
    lane = lax.broadcasted_iota(jnp.int32, (rows, LANES), 1)
    zero = jnp.zeros((rows, LANES), jnp.float32)
    for p in range(own_phis):
        drift_col = cols_ref[p, tilt]
        frac_x = (index_ref[p, tilt] & 7).astype(jnp.float32) / 8.0
        turn = (drift_col + LANES) & (LANES - 1)
        from_left = lane < drift_col
        from_right = lane >= LANES + drift_col
        frame = frames_ref[tilt, p].astype(jnp.float32)
        source = [frame[:, t * LANES : (t + 1) * LANES] for t in range(tiles)] + [zero]
        stepped = [pltpu.roll(s, 1, 1) for s in source[:-1]]
        turned = []
        for t in range(tiles + 1):
            before = stepped[t - 1] if t > 0 else zero
            here = stepped[t] if t < tiles else zero
            mixed = (1.0 - frac_x) * source[t] + frac_x * jnp.where(lane < 1, before, here)
            turned.append(pltpu.roll(mixed, turn, 1))
        moved = []
        for t in range(tiles):
            left = turned[t - 1] if t > 0 else zero
            moved.append(jnp.where(from_left, left, jnp.where(from_right, turned[t + 1], turned[t])))
        for h in range(halves):
            group = jnp.stack(moved[h * SUBS : (h + 1) * SUBS])
            spread_ref[p, PAD_ROWS : PAD_ROWS + rows, h] = jnp.swapaxes(group, 0, 1)
    for p in range(own_phis):
        drift_row = jnp.clip(rows_ref[p, tilt], -MOST_ROWS, MOST_ROWS)
        frac_y = (index_ref[p, tilt] >> 3).astype(jnp.float32) / 8.0
        for r in range(rows):
            row = (1.0 - frac_y) * spread_ref[p, r + PAD_ROWS - drift_row] + frac_y * spread_ref[
                p, r + PAD_ROWS - 1 - drift_row
            ]
            for h in range(halves):
                place = r * halves + h
                staged_ref[place // blocks, place % blocks, tilt, p] = row[h]


def tap_matrices(band):
    spread = 0.8 + 0.6 * band.astype(jnp.float32)
    unnormed = [jnp.exp(-float(k * k) / (2.0 * spread * spread)) for k in range(5)]
    total = unnormed[0] + 2.0 * (unnormed[1] + unnormed[2] + unnormed[3] + unnormed[4])
    taps = [0.125 * (u / total) for u in unnormed]
    made = {}

    def pair(near, far, sign):
        if far > 4:
            return taps[near]
        if (near, far, sign) not in made:
            made[near, far, sign] = taps[near] + sign * taps[far] if near < far else taps[near] * 1.0 + sign * taps[far]
        return made[near, far, sign]

    even = [[pair(abs(p - q), 7 - p - q, 1.0) for q in range(4)] for p in range(4)]
    odd = [[pair(abs(p - q), 7 - p - q, -1.0) for q in range(4)] for p in range(4)]
    return even, odd


def phi_blur(tilts, even, odd):
    plus = [tilts[p] + tilts[7 - p] for p in range(4)]
    minus = [tilts[p] - tilts[7 - p] for p in range(4)]
    halves = []
    for matrix, parts in ((even, plus), (odd, minus)):
        rows = []
        for p in range(4):
            row = matrix[p][0] * parts[0]
            for q in range(1, 4):
                row = row + matrix[p][q] * parts[q]
            rows.append(row)
        halves.append(rows)
    front = [halves[0][p] + halves[1][p] for p in range(4)]
    back = [halves[0][3 - p] - halves[1][3 - p] for p in range(4)]
    return front + back


def cells(data_ref, estimate_ref, blurs_ref, even, odd, emit):
    phis = data_ref.shape[1]

    def blurs(stage, c):
        return [blurs_ref[stage, c, p] for p in range(phis)]

    def keep_blur(stage, c, values, keep=True):
        made = phi_blur(values, even, odd)
        if keep:
            for p in range(phis):
                blurs_ref[stage, c, p] = made[p]
        return made

    def first_estimate(c, add):
        return [data_ref[c, p] + add for p in range(phis)]

    def finish_cell(stage, c, mixed, add, keep=True):
        if stage % 2 == 1:
            made = [data_ref[c, p] / (mixed[p] + 0.1) for p in range(phis)]
        else:
            old = first_estimate(c, add) if stage == 2 else [estimate_ref[c, p] for p in range(phis)]
            made = [o * m for o, m in zip(old, mixed)]
            if stage < STAGES and keep:
                for p in range(phis):
                    estimate_ref[c, p] = made[p]
        if stage < STAGES:
            return keep_blur(stage, c, made, keep)
        emit(c, jnp.swapaxes(jnp.stack(made), 0, 1))
        return made

    return blurs, keep_blur, first_estimate, finish_cell


def run_wave(step, own_tilts, adds, helpers, keep=True):
    blurs, keep_blur, first_estimate, finish_cell = helpers
    tilts = (HALO - 1 - step, HALO + own_tilts + step)
    steps = (1, -1)
    chain = [keep_blur(0, c, first_estimate(c, add), keep) for c, add in zip(tilts, adds)]
    for stage in range(1, STAGES + 1):
        for side in range(2):
            c = tilts[side] + steps[side] * stage
            here, beyond = blurs(stage - 1, c), blurs(stage - 1, c + steps[side])
            mixed = [(x + y) + (y + z) for x, y, z in zip(chain[side], here, beyond)]
            outside = c < HALO if side == 0 else c >= HALO + own_tilts
            chain[side] = finish_cell(stage, c, mixed, jnp.where(outside, adds[side], 0.1), keep)


def end_adds(n_phi):
    phi = lax.axis_index("phi")
    return jnp.where(phi == 0, 0.0, 0.1), jnp.where(phi == n_phi - 1, 0.0, 0.1)


def deliver(n_phi, source_ref, data_ref, estimate_ref, blurs_ref, band_ref, out_hbm, edge_ref, sems, edge_sems):
    tilts, planes = source_ref.shape[:2]
    blocks = planes // SUBS
    copies = []
    for number, (first, size, rows) in enumerate(
        ((1, tilts - 2, planes), (0, 1, planes - SUBS), (tilts - 1, 1, planes - SUBS))
    ):
        at = pl.ds(first, size), pl.ds(0, rows)
        copies.append(pltpu.make_async_copy(source_ref.at[at], out_hbm.at[at], sems.at[number]))
        copies[-1].start()

    def emit(c, made):
        edge_ref[0 if c == HALO else 1] = made

    even, odd = tap_matrices(band_ref[...])
    helpers = cells(data_ref.at[blocks - 1], estimate_ref, blurs_ref, even, odd, emit)
    run_wave(HALO - 1, tilts, end_adds(n_phi), helpers, keep=False)
    for side, t in enumerate((0, tilts - 1)):
        part = pl.ds(planes - SUBS, SUBS)
        copies.append(pltpu.make_async_copy(edge_ref.at[side], out_hbm.at[t, part], edge_sems.at[side]))
        copies[-1].start()
    for copy in copies:
        copy.wait()


def kernel(
    n_phi,
    rows_hbm,
    cols_hbm,
    index_hbm,
    band_hbm,
    frames_hbm,
    out_ref,
    data_ref,
    estimate_ref,
    blurs_ref,
    last_band_ref,
    rows_ref,
    cols_ref,
    index_ref,
    band_ref,
    frames_ref,
    spread_ref,
    staged_ref,
    table_sems,
    band_sem,
    edge_sems,
    middle_sem,
    send_sems,
    recv_sems,
    last_sends,
    last_recvs,
    pair_sends,
    pair_recvs,
    local_sems,
    far_sem,
):
    chi, phi = lax.axis_index("chi"), lax.axis_index("phi")
    other = 1 - chi
    before = lax.rem(phi + n_phi - 1, n_phi)
    after = lax.rem(phi + 1, n_phi)
    has_before, has_after = phi > 0, phi < n_phi - 1
    own_tilts, own_phis = frames_ref.shape[:2]
    blocks, all_tilts, phis = data_ref.shape[:3]
    firsts = (0, own_tilts - HALO)

    def edge_load(tilt, side):
        at = firsts[side] + tilt
        return pltpu.make_async_copy(frames_hbm.at[at], frames_ref.at[at], edge_sems.at[tilt, side])

    barrier = pltpu.get_barrier_semaphore()
    peers = [(before, 0), (before, 1), (after, 0), (after, 1)]

    def greet(to_phi, to_chi):
        pl.semaphore_signal(
            barrier, inc=1, device_id={"chi": to_chi, "phi": to_phi}, device_id_type=pl.DeviceIdType.MESH
        )

    def with_neighbours(act):
        for numbers in ((0, 2), (1, 3)):
            @pl.when(has_before)
            def _():
                act(numbers[0])

            @pl.when(has_after)
            def _():
                act(numbers[1])

    first_chip = (lax.rem(phi, PLANE) == 0).astype(jnp.int32) * has_before.astype(jnp.int32)
    last_chip = (lax.rem(phi, PLANE) == PLANE - 1).astype(jnp.int32)
    told_later = first_chip * (1 - chi)

    @pl.when(has_before)
    def _():
        greet(before, 0)
        greet(before, 1)

    @pl.when(has_after)
    def _():
        @pl.when(last_chip == 0)
        def _():
            greet(after, 0)

        greet(after, 1)

    greet(phi, other)
    greetings = 1 + 2 * (has_before.astype(jnp.int32) - told_later) + 2 * has_after.astype(jnp.int32)

    tables = ((rows_hbm, rows_ref), (cols_hbm, cols_ref), (index_hbm, index_ref))
    table_loads = [pltpu.make_async_copy(a, b, table_sems.at[i]) for i, (a, b) in enumerate(tables)]
    for load in table_loads:
        load.start()
    for tilt in range(HALO):
        for side in (1, 0):
            edge_load(tilt, side).start()
    inner = pl.ds(HALO, own_tilts - 2 * HALO)
    middle_load = pltpu.make_async_copy(frames_hbm.at[inner], frames_ref.at[inner], middle_sem)
    middle_load.start()
    band_load = pltpu.make_async_copy(band_hbm, band_ref, band_sem)
    band_load.start()

    empty = jnp.zeros(spread_ref.shape[2:], jnp.float32)
    for p in range(own_phis):
        for r in range(PAD_ROWS):
            spread_ref[p, r] = empty
            spread_ref[p, spread_ref.shape[1] - 1 - r] = empty

    mine = pl.ds(chi * own_phis, own_phis)

    def neighbour_copy(b, number, tilt, tilts, send_sem, recv_sem, flip):
        back = number < 2
        to_chi = lax.rem(flip + number, 2)
        first = 0 if back else own_tilts - HALO
        first_there = all_tilts - HALO if back else 0
        return pltpu.make_async_remote_copy(
            src_ref=staged_ref.at[to_chi, b, pl.ds(first + tilt, tilts)],
            dst_ref=data_ref.at[b, pl.ds(first_there + tilt, tilts), mine],
            send_sem=send_sem,
            recv_sem=recv_sem,
            device_id={"chi": to_chi, "phi": before if back else after},
            device_id_type=pl.DeviceIdType.MESH,
        )

    def place_of(number):
        return (0 if number < 2 else 2) + chi

    def halo_copy(b, number, tilt=0, tilts=HALO):
        return neighbour_copy(b, number, tilt, tilts, send_sems.at[b, number], recv_sems.at[b, place_of(number)], b)

    def last_copy(number, step):
        tilt = step if number < 2 else HALO - 1 - step
        return neighbour_copy(
            blocks - 1, number, tilt, 1, last_sends.at[number, step], last_recvs.at[place_of(number), step], step
        )

    def arrival(b, place, tilt, tilts, recv_sem):
        back = place < 2
        from_chi = place % 2
        first = all_tilts - HALO if back else 0
        return pltpu.make_async_remote_copy(
            src_ref=staged_ref.at[0, b, pl.ds(0, tilts)],
            dst_ref=data_ref.at[b, pl.ds(first + tilt, tilts), pl.ds(from_chi * own_phis, own_phis)],
            send_sem=send_sems.at[0, place],
            recv_sem=recv_sem,
            device_id={"chi": from_chi, "phi": after if back else before},
            device_id_type=pl.DeviceIdType.MESH,
        )

    middle = pl.ds(HALO, own_tilts)

    def pair_copy(b, phis_at):
        return pltpu.make_async_remote_copy(
            src_ref=staged_ref.at[other, b],
            dst_ref=data_ref.at[b, middle, phis_at],
            send_sem=pair_sends.at[b],
            recv_sem=pair_recvs.at[b],
            device_id={"chi": other, "phi": phi},
            device_id_type=pl.DeviceIdType.MESH,
        )

    def local_copy(b):
        return pltpu.make_async_copy(staged_ref.at[chi, b], data_ref.at[b, middle, mine], local_sems.at[b])

    def shift_at(tilt):
        shift_tilt(tilt, rows_ref, cols_ref, index_ref, frames_ref, spread_ref, staged_ref)

    for load in table_loads:
        load.wait()

    def to_before(act, also):
        @pl.when(has_before)
        def _():
            @pl.when(also)
            def _():
                act(0)
                act(1)

    def to_after(act):
        @pl.when(has_after)
        def _():
            act(2)
            act(3)

    def shift_edge(tilt, side):
        edge_load(tilt, side).wait()
        shift_at(firsts[side] + tilt)

    def shift_edges(tilt, carry):
        shift_edge(tilt, 1)

        @pl.when(tilt == 0)
        def _():
            pl.semaphore_wait(barrier, greetings)

            @pl.when(first_chip * chi == 1)
            def _():
                pl.semaphore_signal(
                    far_sem, inc=1, device_id={"chi": other, "phi": phi}, device_id_type=pl.DeviceIdType.MESH
                )

        to_after(lambda number: halo_copy(0, number, tilt, 1).start())
        shift_edge(tilt, 0)
        to_before(lambda number: halo_copy(0, number, tilt, 1).start(), told_later == 0)
        return carry

    lax.fori_loop(0, HALO, shift_edges, 0)

    def send_halos(b, carry):
        with_neighbours(lambda number: halo_copy(b, number).start())
        return carry

    def send_after(b, carry):
        to_after(lambda number: halo_copy(b, number).start())
        return carry

    def send_before(b, carry):
        to_before(lambda number: halo_copy(b, number).start(), True)
        return carry

    @pl.when(told_later == 0)
    def _():
        lax.fori_loop(1, EARLY, send_halos, 0)

    @pl.when(told_later == 1)
    def _():
        lax.fori_loop(1, EARLY, send_after, 0)
        pl.semaphore_wait(far_sem, 1)
        lax.fori_loop(0, EARLY, send_before, 0)

    lax.fori_loop(EARLY, blocks - 1, send_halos, 0)

    def send_last(step, carry):
        with_neighbours(lambda number: last_copy(number, step).start())
        return carry

    lax.fori_loop(0, HALO, send_last, 0)
    middle_load.wait()

    def shift_inner(tilt, carry):
        shift_at(tilt)
        return carry

    lax.fori_loop(HALO, own_tilts - HALO, shift_inner, 0)

    def send_pairs(b, carry):
        pair_copy(b, mine).start()
        local_copy(b).start()
        return carry

    lax.fori_loop(0, blocks, send_pairs, 0)
    band_load.wait()

    adds = end_adds(n_phi)

    def block(b, last):
        even, odd = tap_matrices(band_ref[pl.ds(pl.multiple_of(b * SUBS, SUBS), SUBS), :])
        rows_at = pl.ds(pl.multiple_of(b * SUBS, SUBS), SUBS)

        def emit(c, made):
            out_ref[c - HALO, rows_at] = made

        blurs, keep_blur, first_estimate, finish_cell = cells(
            data_ref.at[b], estimate_ref, blurs_ref, even, odd, emit
        )

        pair_copy(b, pl.ds(other * own_phis, own_phis)).wait_recv()
        local_copy(b).wait()

        def start_cell(c, carry):
            keep_blur(0, c, first_estimate(c, 0.1))
            return carry

        lax.fori_loop(HALO, HALO + own_tilts, start_cell, 0, unroll=2)
        for stage in range(1, STAGES + 1):
            low, high = HALO + stage, HALO + own_tilts - stage

            def cell(c, carry):
                here, joined = carry
                beyond = blurs(stage - 1, c + 1)
                ahead = [x + y for x, y in zip(here, beyond)]
                finish_cell(stage, c, [x + y for x, y in zip(joined, ahead)], 0.1)
                return beyond, ahead

            near, here = blurs(stage - 1, low - 1), blurs(stage - 1, low)
            lax.fori_loop(low, high, cell, (here, [x + y for x, y in zip(near, here)]), unroll=2)

        nothing = jnp.zeros(data_ref.shape[2:], jnp.float32)

        @pl.when(phi == 0)
        def _():
            for c in range(HALO):
                data_ref[b, c] = nothing

        @pl.when(phi == n_phi - 1)
        def _():
            for c in range(all_tilts - HALO, all_tilts):
                data_ref[b, c] = nothing

        def wait_for(places, back_tilt, step):
            for place in places:
                if last:
                    arrival(b, place, back_tilt, 1, last_recvs.at[place, step]).wait_recv()
                else:
                    arrival(b, place, 0, HALO, recv_sems.at[b, place]).wait_recv()

        def wait_step(step):
            @pl.when(has_before)
            def _():
                wait_for((2, 3), HALO - 1 - step, step)

            @pl.when(has_after)
            def _():
                wait_for((0, 1), step, step)

        if not last:
            wait_step(0)

        helpers = blurs, keep_blur, first_estimate, finish_cell

        def wave(step, carry):
            if last:
                wait_step(step)
            run_wave(step, own_tilts, adds, helpers)
            return carry

        lax.fori_loop(0, HALO - 1 if last else HALO, wave, 0)
        if last:
            last_band_ref[...] = band_ref[rows_at, :]
            wait_step(HALO - 1)

    def some_block(b, carry):
        block(b, False)
        return carry

    lax.fori_loop(0, blocks - 1, some_block, 0)
    block(blocks - 1, True)

    def finish(b, carry):
        with_neighbours(lambda number: halo_copy(b, number).wait_send())
        return carry

    lax.fori_loop(0, blocks - 1, finish, 0)

    def finish_last(step, carry):
        with_neighbours(lambda number: last_copy(number, step).wait_send())
        return carry

    lax.fori_loop(0, HALO, finish_last, 0)

    def finish_pair(b, carry):
        pair_copy(b, mine).wait_send()
        return carry

    lax.fori_loop(0, blocks, finish_pair, 0)


def body(n_phi, frames, drift_rows, drift_cols, weight_index, blur_band):
    tilts, own_phis, rows, cols = frames.shape
    pixels = blur_band.shape[0]
    phis = 2 * own_phis
    planes = pixels // LANES
    blocks = planes // SUBS
    tile = (SUBS, LANES)
    all_tilts = tilts + 2 * HALO
    hbm = pl.BlockSpec(memory_space=pltpu.HBM)
    table = pltpu.SMEM((own_phis, tilts), jnp.int32)
    vmem = pl.BlockSpec(memory_space=pltpu.VMEM)
    held = pl.pallas_call(
        functools.partial(kernel, n_phi),
        out_shape=(
            pltpu.VMEM((tilts, planes, phis, LANES), jnp.float32),
            pltpu.VMEM((blocks, all_tilts, phis) + tile, jnp.float32),
            pltpu.VMEM((all_tilts, phis) + tile, jnp.float32),
            pltpu.VMEM((STAGES, all_tilts, phis) + tile, jnp.float32),
            pltpu.VMEM(tile, jnp.int32),
        ),
        in_specs=[hbm] * 5,
        out_specs=(vmem,) * 5,
        scratch_shapes=[
            table,
            table,
            table,
            pltpu.VMEM((planes, LANES), jnp.int32),
            pltpu.VMEM(frames.shape, frames.dtype),
            pltpu.VMEM((own_phis, rows + 2 * PAD_ROWS, cols // LANES // SUBS) + tile, jnp.float32),
            pltpu.VMEM((2, blocks, tilts, own_phis) + tile, jnp.float32),
            pltpu.SemaphoreType.DMA((3,)),
            pltpu.SemaphoreType.DMA,
            pltpu.SemaphoreType.DMA((HALO, 2)),
            pltpu.SemaphoreType.DMA,
            pltpu.SemaphoreType.DMA((blocks - 1, REMOTE)),
            pltpu.SemaphoreType.DMA((blocks - 1, REMOTE)),
            pltpu.SemaphoreType.DMA((REMOTE, HALO)),
            pltpu.SemaphoreType.DMA((REMOTE, HALO)),
            pltpu.SemaphoreType.DMA((blocks,)),
            pltpu.SemaphoreType.DMA((blocks,)),
            pltpu.SemaphoreType.DMA((blocks,)),
            pltpu.SemaphoreType.REGULAR,
        ],
        compiler_params=pltpu.CompilerParams(
            collective_id=0, has_side_effects=True, vmem_limit_bytes=45 * 1024 * 1024
        ),
        name="rocking",
    )(drift_rows.T, drift_cols.T, weight_index.T, blur_band.reshape(planes, LANES), frames)
    held = [pltpu.with_memory_space_constraint(part, pltpu.VMEM) for part in held]
    out = pl.pallas_call(
        functools.partial(deliver, n_phi),
        out_shape=jax.ShapeDtypeStruct((tilts, planes, phis, LANES), jnp.float32),
        in_specs=[vmem] * 5,
        out_specs=hbm,
        scratch_shapes=[
            pltpu.VMEM((2, SUBS, phis, LANES), jnp.float32),
            pltpu.SemaphoreType.DMA((3,)),
            pltpu.SemaphoreType.DMA((2,)),
        ],
        compiler_params=pltpu.CompilerParams(vmem_limit_bytes=16 * 1024 * 1024),
        name="deliver",
    )(*held)
    return out.transpose(0, 2, 1, 3).reshape(tilts, phis, pixels)


def solution(mesh):
    return jax.shard_map(
        functools.partial(body, mesh.shape["phi"]),
        mesh=mesh,
        in_specs=(
            P("phi", "chi", None, None),
            P("phi", "chi"),
            P("phi", "chi"),
            P("phi", "chi"),
            P("chi"),
        ),
        out_specs=P("phi", None, "chi"),
        check_vma=False,
    )
```

```python
import functools

import jax
import jax.numpy as jnp
from jax import lax
from jax.experimental import pallas as pl
from jax.experimental.pallas import tpu as pltpu
from jax.sharding import PartitionSpec as P

ITERS = 3
STAGES = 2 * ITERS
HALO = STAGES
LANES = 128
SUBS = 8
MOST_ROWS = 2
PAD_ROWS = MOST_ROWS + 1
PLANE = 16
EARLY = 1
REMOTE = 4


def shift_tilt(tilt, rows_ref, cols_ref, index_ref, frames_ref, spread_ref, staged_ref):
    own_phis, rows, cols = frames_ref.shape[1:]
    tiles = cols // LANES
    halves = tiles // SUBS
    blocks = staged_ref.shape[1]
    lane = lax.broadcasted_iota(jnp.int32, (rows, LANES), 1)
    zero = jnp.zeros((rows, LANES), jnp.float32)
    for p in range(own_phis):
        drift_col = cols_ref[p, tilt]
        frac_x = (index_ref[p, tilt] & 7).astype(jnp.float32) / 8.0
        turn = (drift_col + LANES) & (LANES - 1)
        from_left = lane < drift_col
        from_right = lane >= LANES + drift_col
        frame = frames_ref[tilt, p].astype(jnp.float32)
        source = [frame[:, t * LANES : (t + 1) * LANES] for t in range(tiles)] + [zero]
        stepped = [pltpu.roll(s, 1, 1) for s in source[:-1]]
        turned = []
        for t in range(tiles + 1):
            before = stepped[t - 1] if t > 0 else zero
            here = stepped[t] if t < tiles else zero
            mixed = (1.0 - frac_x) * source[t] + frac_x * jnp.where(lane < 1, before, here)
            turned.append(pltpu.roll(mixed, turn, 1))
        moved = []
        for t in range(tiles):
            left = turned[t - 1] if t > 0 else zero
            moved.append(jnp.where(from_left, left, jnp.where(from_right, turned[t + 1], turned[t])))
        for h in range(halves):
            group = jnp.stack(moved[h * SUBS : (h + 1) * SUBS])
            spread_ref[p, PAD_ROWS : PAD_ROWS + rows, h] = jnp.swapaxes(group, 0, 1)
    for p in range(own_phis):
        drift_row = jnp.clip(rows_ref[p, tilt], -MOST_ROWS, MOST_ROWS)
        frac_y = (index_ref[p, tilt] >> 3).astype(jnp.float32) / 8.0
        for r in range(rows):
            row = (1.0 - frac_y) * spread_ref[p, r + PAD_ROWS - drift_row] + frac_y * spread_ref[
                p, r + PAD_ROWS - 1 - drift_row
            ]
            for h in range(halves):
                place = r * halves + h
                staged_ref[place // blocks, place % blocks, tilt, p] = row[h]


def tap_matrices(band):
    spread = 0.8 + 0.6 * band.astype(jnp.float32)
    unnormed = [jnp.exp(-float(k * k) / (2.0 * spread * spread)) for k in range(5)]
    total = unnormed[0] + 2.0 * (unnormed[1] + unnormed[2] + unnormed[3] + unnormed[4])
    taps = [0.125 * (u / total) for u in unnormed]
    made = {}

    def pair(near, far, sign):
        if far > 4:
            return taps[near]
        if (near, far, sign) not in made:
            made[near, far, sign] = taps[near] + sign * taps[far] if near < far else taps[near] * 1.0 + sign * taps[far]
        return made[near, far, sign]

    even = [[pair(abs(p - q), 7 - p - q, 1.0) for q in range(4)] for p in range(4)]
    odd = [[pair(abs(p - q), 7 - p - q, -1.0) for q in range(4)] for p in range(4)]
    return even, odd


def phi_blur(tilts, even, odd):
    plus = [tilts[p] + tilts[7 - p] for p in range(4)]
    minus = [tilts[p] - tilts[7 - p] for p in range(4)]
    halves = []
    for matrix, parts in ((even, plus), (odd, minus)):
        rows = []
        for p in range(4):
            row = matrix[p][0] * parts[0]
            for q in range(1, 4):
                row = row + matrix[p][q] * parts[q]
            rows.append(row)
        halves.append(rows)
    front = [halves[0][p] + halves[1][p] for p in range(4)]
    back = [halves[0][3 - p] - halves[1][3 - p] for p in range(4)]
    return front + back


def cells(data_ref, estimate_ref, blurs_ref, even, odd, emit):
    phis = data_ref.shape[1]

    def blurs(stage, c):
        return [blurs_ref[stage, c, p] for p in range(phis)]

    def keep_blur(stage, c, values, keep=True):
        made = phi_blur(values, even, odd)
        if keep:
            for p in range(phis):
                blurs_ref[stage, c, p] = made[p]
        return made

    def first_estimate(c, add):
        return [data_ref[c, p] + add for p in range(phis)]

    def finish_cell(stage, c, mixed, add, keep=True):
        if stage % 2 == 1:
            made = [data_ref[c, p] / (mixed[p] + 0.1) for p in range(phis)]
        else:
            old = first_estimate(c, add) if stage == 2 else [estimate_ref[c, p] for p in range(phis)]
            made = [o * m for o, m in zip(old, mixed)]
            if stage < STAGES and keep:
                for p in range(phis):
                    estimate_ref[c, p] = made[p]
        if stage < STAGES:
            return keep_blur(stage, c, made, keep)
        emit(c, jnp.swapaxes(jnp.stack(made), 0, 1))
        return made

    return blurs, keep_blur, first_estimate, finish_cell


def run_wave(step, own_tilts, adds, helpers, keep=True):
    blurs, keep_blur, first_estimate, finish_cell = helpers
    tilts = (HALO - 1 - step, HALO + own_tilts + step)
    steps = (1, -1)
    chain = [keep_blur(0, c, first_estimate(c, add), keep) for c, add in zip(tilts, adds)]
    for stage in range(1, STAGES + 1):
        for side in range(2):
            c = tilts[side] + steps[side] * stage
            here, beyond = blurs(stage - 1, c), blurs(stage - 1, c + steps[side])
            mixed = [(x + y) + (y + z) for x, y, z in zip(chain[side], here, beyond)]
            outside = c < HALO if side == 0 else c >= HALO + own_tilts
            chain[side] = finish_cell(stage, c, mixed, jnp.where(outside, adds[side], 0.1), keep)


def end_adds(n_phi):
    phi = lax.axis_index("phi")
    return jnp.where(phi == 0, 0.0, 0.1), jnp.where(phi == n_phi - 1, 0.0, 0.1)


def deliver(n_phi, source_ref, data_ref, estimate_ref, blurs_ref, band_ref, out_hbm, edge_ref, sems, edge_sems):
    tilts, planes = source_ref.shape[:2]
    blocks = planes // SUBS
    copies = []
    for number, (first, size, rows) in enumerate(
        ((1, tilts - 2, planes), (0, 1, planes - SUBS), (tilts - 1, 1, planes - SUBS))
    ):
        at = pl.ds(first, size), pl.ds(0, rows)
        copies.append(pltpu.make_async_copy(source_ref.at[at], out_hbm.at[at], sems.at[number]))
        copies[-1].start()

    def emit(c, made):
        edge_ref[0 if c == HALO else 1] = made

    even, odd = tap_matrices(band_ref[...])
    helpers = cells(data_ref.at[blocks - 1], estimate_ref, blurs_ref, even, odd, emit)
    run_wave(HALO - 1, tilts, end_adds(n_phi), helpers, keep=False)
    for side, t in enumerate((0, tilts - 1)):
        part = pl.ds(planes - SUBS, SUBS)
        copies.append(pltpu.make_async_copy(edge_ref.at[side], out_hbm.at[t, part], edge_sems.at[side]))
        copies[-1].start()
    for copy in copies:
        copy.wait()


def kernel(
    n_phi,
    rows_hbm,
    cols_hbm,
    index_hbm,
    band_hbm,
    frames_hbm,
    out_ref,
    data_ref,
    estimate_ref,
    blurs_ref,
    last_band_ref,
    rows_ref,
    cols_ref,
    index_ref,
    band_ref,
    frames_ref,
    spread_ref,
    staged_ref,
    table_sems,
    band_sem,
    edge_sems,
    middle_sem,
    send_sems,
    recv_sems,
    last_sends,
    last_recvs,
    pair_sends,
    pair_recvs,
    local_sems,
    far_sem,
):
    chi, phi = lax.axis_index("chi"), lax.axis_index("phi")
    other = 1 - chi
    before = lax.rem(phi + n_phi - 1, n_phi)
    after = lax.rem(phi + 1, n_phi)
    has_before, has_after = phi > 0, phi < n_phi - 1
    own_tilts, own_phis = frames_ref.shape[:2]
    blocks, all_tilts, phis = data_ref.shape[:3]
    firsts = (0, own_tilts - HALO)

    def edge_load(tilt, side):
        at = firsts[side] + tilt
        return pltpu.make_async_copy(frames_hbm.at[at], frames_ref.at[at], edge_sems.at[tilt, side])

    barrier = pltpu.get_barrier_semaphore()
    peers = [(before, 0), (before, 1), (after, 0), (after, 1)]

    def greet(to_phi, to_chi):
        pl.semaphore_signal(
            barrier, inc=1, device_id={"chi": to_chi, "phi": to_phi}, device_id_type=pl.DeviceIdType.MESH
        )

    def with_neighbours(act):
        for numbers in ((0, 2), (1, 3)):
            @pl.when(has_before)
            def _():
                act(numbers[0])

            @pl.when(has_after)
            def _():
                act(numbers[1])

    first_chip = (lax.rem(phi, PLANE) == 0).astype(jnp.int32) * has_before.astype(jnp.int32)
    last_chip = (lax.rem(phi, PLANE) == PLANE - 1).astype(jnp.int32)
    told_later = first_chip * (1 - chi)

    @pl.when(has_before)
    def _():
        greet(before, 0)
        greet(before, 1)

    @pl.when(has_after)
    def _():
        @pl.when(last_chip == 0)
        def _():
            greet(after, 0)

        greet(after, 1)

    greet(phi, other)
    greetings = 1 + 2 * (has_before.astype(jnp.int32) - told_later) + 2 * has_after.astype(jnp.int32)

    tables = ((rows_hbm, rows_ref), (cols_hbm, cols_ref), (index_hbm, index_ref))
    table_loads = [pltpu.make_async_copy(a, b, table_sems.at[i]) for i, (a, b) in enumerate(tables)]
    for load in table_loads:
        load.start()
    for tilt in range(HALO):
        for side in (1, 0):
            edge_load(tilt, side).start()
    inner = pl.ds(HALO, own_tilts - 2 * HALO)
    middle_load = pltpu.make_async_copy(frames_hbm.at[inner], frames_ref.at[inner], middle_sem)
    middle_load.start()
    band_load = pltpu.make_async_copy(band_hbm, band_ref, band_sem)
    band_load.start()

    empty = jnp.zeros(spread_ref.shape[2:], jnp.float32)
    for p in range(own_phis):
        for r in range(PAD_ROWS):
            spread_ref[p, r] = empty
            spread_ref[p, spread_ref.shape[1] - 1 - r] = empty

    mine = pl.ds(chi * own_phis, own_phis)

    def neighbour_copy(b, number, tilt, tilts, send_sem, recv_sem, flip):
        back = number < 2
        to_chi = lax.rem(flip + number, 2)
        first = 0 if back else own_tilts - HALO
        first_there = all_tilts - HALO if back else 0
        return pltpu.make_async_remote_copy(
            src_ref=staged_ref.at[to_chi, b, pl.ds(first + tilt, tilts)],
            dst_ref=data_ref.at[b, pl.ds(first_there + tilt, tilts), mine],
            send_sem=send_sem,
            recv_sem=recv_sem,
            device_id={"chi": to_chi, "phi": before if back else after},
            device_id_type=pl.DeviceIdType.MESH,
        )

    def place_of(number):
        return (0 if number < 2 else 2) + chi

    def halo_copy(b, number, tilt=0, tilts=HALO):
        return neighbour_copy(b, number, tilt, tilts, send_sems.at[b, number], recv_sems.at[b, place_of(number)], b)

    def last_copy(number, step):
        tilt = step if number < 2 else HALO - 1 - step
        return neighbour_copy(
            blocks - 1, number, tilt, 1, last_sends.at[number, step], last_recvs.at[place_of(number), step], step
        )

    def arrival(b, place, tilt, tilts, recv_sem):
        back = place < 2
        from_chi = place % 2
        first = all_tilts - HALO if back else 0
        return pltpu.make_async_remote_copy(
            src_ref=staged_ref.at[0, b, pl.ds(0, tilts)],
            dst_ref=data_ref.at[b, pl.ds(first + tilt, tilts), pl.ds(from_chi * own_phis, own_phis)],
            send_sem=send_sems.at[0, place],
            recv_sem=recv_sem,
            device_id={"chi": from_chi, "phi": after if back else before},
            device_id_type=pl.DeviceIdType.MESH,
        )

    middle = pl.ds(HALO, own_tilts)

    def pair_copy(b, phis_at):
        return pltpu.make_async_remote_copy(
            src_ref=staged_ref.at[other, b],
            dst_ref=data_ref.at[b, middle, phis_at],
            send_sem=pair_sends.at[b],
            recv_sem=pair_recvs.at[b],
            device_id={"chi": other, "phi": phi},
            device_id_type=pl.DeviceIdType.MESH,
        )

    def local_copy(b):
        return pltpu.make_async_copy(staged_ref.at[chi, b], data_ref.at[b, middle, mine], local_sems.at[b])

    def shift_at(tilt):
        shift_tilt(tilt, rows_ref, cols_ref, index_ref, frames_ref, spread_ref, staged_ref)

    for load in table_loads:
        load.wait()

    def to_before(act, also):
        @pl.when(has_before)
        def _():
            @pl.when(also)
            def _():
                act(0)
                act(1)

    def to_after(act):
        @pl.when(has_after)
        def _():
            act(2)
            act(3)

    def shift_edge(tilt, side):
        edge_load(tilt, side).wait()
        shift_at(firsts[side] + tilt)

    def shift_edges(tilt, carry):
        shift_edge(tilt, 1)

        @pl.when(tilt == 0)
        def _():
            pl.semaphore_wait(barrier, greetings)

            @pl.when(first_chip * chi == 1)
            def _():
                pl.semaphore_signal(
                    far_sem, inc=1, device_id={"chi": other, "phi": phi}, device_id_type=pl.DeviceIdType.MESH
                )

        to_after(lambda number: halo_copy(0, number, tilt, 1).start())
        shift_edge(tilt, 0)
        to_before(lambda number: halo_copy(0, number, tilt, 1).start(), told_later == 0)
        return carry

    lax.fori_loop(0, HALO, shift_edges, 0)

    def send_halos(b, carry):
        with_neighbours(lambda number: halo_copy(b, number).start())
        return carry

    def send_after(b, carry):
        to_after(lambda number: halo_copy(b, number).start())
        return carry

    def send_before(b, carry):
        to_before(lambda number: halo_copy(b, number).start(), True)
        return carry

    @pl.when(told_later == 0)
    def _():
        lax.fori_loop(1, EARLY, send_halos, 0)

    @pl.when(told_later == 1)
    def _():
        lax.fori_loop(1, EARLY, send_after, 0)
        pl.semaphore_wait(far_sem, 1)
        lax.fori_loop(0, EARLY, send_before, 0)

    lax.fori_loop(EARLY, blocks - 1, send_halos, 0)

    def send_last(step, carry):
        with_neighbours(lambda number: last_copy(number, step).start())
        return carry

    lax.fori_loop(0, HALO, send_last, 0)
    middle_load.wait()

    def shift_inner(tilt, carry):
        shift_at(tilt)
        return carry

    lax.fori_loop(HALO, own_tilts - HALO, shift_inner, 0)

    def send_pairs(b, carry):
        pair_copy(b, mine).start()
        local_copy(b).start()
        return carry

    lax.fori_loop(0, blocks, send_pairs, 0)
    band_load.wait()

    adds = end_adds(n_phi)

    def block(b, last):
        even, odd = tap_matrices(band_ref[pl.ds(pl.multiple_of(b * SUBS, SUBS), SUBS), :])
        rows_at = pl.ds(pl.multiple_of(b * SUBS, SUBS), SUBS)

        def emit(c, made):
            out_ref[c - HALO, rows_at] = made

        blurs, keep_blur, first_estimate, finish_cell = cells(
            data_ref.at[b], estimate_ref, blurs_ref, even, odd, emit
        )

        pair_copy(b, pl.ds(other * own_phis, own_phis)).wait_recv()
        local_copy(b).wait()

        def start_cell(c, carry):
            keep_blur(0, c, first_estimate(c, 0.1))
            return carry

        lax.fori_loop(HALO, HALO + own_tilts, start_cell, 0, unroll=2)
        for stage in range(1, STAGES + 1):
            low, high = HALO + stage, HALO + own_tilts - stage

            def cell(c, carry):
                here, joined = carry
                beyond = blurs(stage - 1, c + 1)
                ahead = [x + y for x, y in zip(here, beyond)]
                finish_cell(stage, c, [x + y for x, y in zip(joined, ahead)], 0.1)
                return beyond, ahead

            near, here = blurs(stage - 1, low - 1), blurs(stage - 1, low)
            lax.fori_loop(low, high, cell, (here, [x + y for x, y in zip(near, here)]), unroll=2)

        nothing = jnp.zeros(data_ref.shape[2:], jnp.float32)

        @pl.when(phi == 0)
        def _():
            for c in range(HALO):
                data_ref[b, c] = nothing

        @pl.when(phi == n_phi - 1)
        def _():
            for c in range(all_tilts - HALO, all_tilts):
                data_ref[b, c] = nothing

        def wait_for(places, back_tilt, step):
            for place in places:
                if last:
                    arrival(b, place, back_tilt, 1, last_recvs.at[place, step]).wait_recv()
                else:
                    arrival(b, place, 0, HALO, recv_sems.at[b, place]).wait_recv()

        def wait_step(step):
            @pl.when(has_before)
            def _():
                wait_for((2, 3), HALO - 1 - step, step)

            @pl.when(has_after)
            def _():
                wait_for((0, 1), step, step)

        if not last:
            wait_step(0)

        helpers = blurs, keep_blur, first_estimate, finish_cell

        def wave(step, carry):
            if last:
                wait_step(step)
            run_wave(step, own_tilts, adds, helpers)
            return carry

        lax.fori_loop(0, HALO - 1 if last else HALO, wave, 0)
        if last:
            last_band_ref[...] = band_ref[rows_at, :]
            wait_step(HALO - 1)

    def some_block(b, carry):
        block(b, False)
        return carry

    lax.fori_loop(0, blocks - 1, some_block, 0)
    block(blocks - 1, True)

    def finish(b, carry):
        with_neighbours(lambda number: halo_copy(b, number).wait_send())
        return carry

    lax.fori_loop(0, blocks - 1, finish, 0)

    def finish_last(step, carry):
        with_neighbours(lambda number: last_copy(number, step).wait_send())
        return carry

    lax.fori_loop(0, HALO, finish_last, 0)

    def finish_pair(b, carry):
        pair_copy(b, mine).wait_send()
        return carry

    lax.fori_loop(0, blocks, finish_pair, 0)


def body(n_phi, frames, drift_rows, drift_cols, weight_index, blur_band):
    tilts, own_phis, rows, cols = frames.shape
    pixels = blur_band.shape[0]
    phis = 2 * own_phis
    planes = pixels // LANES
    blocks = planes // SUBS
    tile = (SUBS, LANES)
    all_tilts = tilts + 2 * HALO
    hbm = pl.BlockSpec(memory_space=pltpu.HBM)
    table = pltpu.SMEM((own_phis, tilts), jnp.int32)
    vmem = pl.BlockSpec(memory_space=pltpu.VMEM)
    held = pl.pallas_call(
        functools.partial(kernel, n_phi),
        out_shape=(
            pltpu.VMEM((tilts, planes, phis, LANES), jnp.float32),
            pltpu.VMEM((blocks, all_tilts, phis) + tile, jnp.float32),
            pltpu.VMEM((all_tilts, phis) + tile, jnp.float32),
            pltpu.VMEM((STAGES, all_tilts, phis) + tile, jnp.float32),
            pltpu.VMEM(tile, jnp.int32),
        ),
        in_specs=[hbm] * 5,
        out_specs=(vmem,) * 5,
        scratch_shapes=[
            table,
            table,
            table,
            pltpu.VMEM((planes, LANES), jnp.int32),
            pltpu.VMEM(frames.shape, frames.dtype),
            pltpu.VMEM((own_phis, rows + 2 * PAD_ROWS, cols // LANES // SUBS) + tile, jnp.float32),
            pltpu.VMEM((2, blocks, tilts, own_phis) + tile, jnp.float32),
            pltpu.SemaphoreType.DMA((3,)),
            pltpu.SemaphoreType.DMA,
            pltpu.SemaphoreType.DMA((HALO, 2)),
            pltpu.SemaphoreType.DMA,
            pltpu.SemaphoreType.DMA((blocks - 1, REMOTE)),
            pltpu.SemaphoreType.DMA((blocks - 1, REMOTE)),
            pltpu.SemaphoreType.DMA((REMOTE, HALO)),
            pltpu.SemaphoreType.DMA((REMOTE, HALO)),
            pltpu.SemaphoreType.DMA((blocks,)),
            pltpu.SemaphoreType.DMA((blocks,)),
            pltpu.SemaphoreType.DMA((blocks,)),
            pltpu.SemaphoreType.REGULAR,
        ],
        compiler_params=pltpu.CompilerParams(
            collective_id=0, has_side_effects=True, vmem_limit_bytes=45 * 1024 * 1024
        ),
        name="rocking",
    )(drift_rows.T, drift_cols.T, weight_index.T, blur_band.reshape(planes, LANES), frames)
    held = [pltpu.with_memory_space_constraint(part, pltpu.VMEM) for part in held]
    out = pl.pallas_call(
        functools.partial(deliver, n_phi),
        out_shape=jax.ShapeDtypeStruct((tilts, planes, phis, LANES), jnp.float32),
        in_specs=[vmem] * 5,
        out_specs=hbm,
        scratch_shapes=[
            pltpu.VMEM((2, SUBS, phis, LANES), jnp.float32),
            pltpu.SemaphoreType.DMA((3,)),
            pltpu.SemaphoreType.DMA((2,)),
        ],
        compiler_params=pltpu.CompilerParams(vmem_limit_bytes=16 * 1024 * 1024),
        name="deliver",
    )(*held)
    return out.transpose(0, 2, 1, 3).reshape(tilts, phis, pixels)


def solution(mesh):
    return jax.shard_map(
        functools.partial(body, mesh.shape["phi"]),
        mesh=mesh,
        in_specs=(
            P("phi", "chi", None, None),
            P("phi", "chi"),
            P("phi", "chi"),
            P("phi", "chi"),
            P("chi"),
        ),
        out_specs=P("phi", None, "chi"),
        check_vma=False,
    )
```
